32 devices in a mesh: req: 4 (over y, core), seq: 8 (over z, x).
Axes of the slice: x: 2, y: 2, z: 4, core: 2. Of those that a mesh axis runs over, the one named last changes fastest.
Arguments:
- embedded: bfloat16 [4, 48, 3584], P(None, 'req'), may hold values from -6 to 6
- cache_keys: bfloat16 [4, 4096, 2048], P('req', 'seq'), may hold values from -6 to 6
- cache_values: bfloat16 [4, 4096, 2048], P('req', 'seq'), may hold values from -6 to 6
- token_owner: int32 [4, 4096], P('req', 'seq'), may hold values from 0 to 11, as said below
- dealing: int32 [48], replicated, may hold values from 0 to 47, as said below
- lengths: int32 [48], replicated, may hold values from 1 to 2048, as said below
- project_weight: bfloat16 [3584, 8192], P(None, 'seq')
- output_weight: bfloat16 [4096, 3584], P('seq'), may hold values from -0.09375 to 0.09375
- gate_weight: bfloat16 [3584, 14336], P(None, ('req', 'seq')), may hold values from -0.09375 to 0.09375
- up_weight: bfloat16 [3584, 14336], P(None, ('req', 'seq')), may hold values from -0.09375 to 0.09375
- down_weight: bfloat16 [14336, 3584], P(('req', 'seq')), may hold values from -0.046875 to 0.046875
- gain_first: float32 [3584], replicated, may hold values from 0.1 to 1.9
- gain_second: float32 [3584], replicated, may hold values from 0.1 to 1.9
- gain_third: float32 [3584], replicated, may hold values from 0.1 to 1.9
- gain_fourth: float32 [3584], replicated, may hold values from 0.1 to 1.9
Outputs:
- results: bfloat16 [4, 48, 3584], P(None, 'req')
The draws below stay inside these ranges and needn't reach their ends.
Inputs may be any that keep to these rules, and one draw needn't show every extreme that they name: A permutation of the requests; slot i of req group g serves request dealing[g * 12 + i]. The lengths of the 12 requests dealt to one group sum to 4096; in every group the longest is exactly 2048. `token_owner`: each slot owns a contiguous run of its group's pool, runs in slot order, as many tokens as its request's length.
All inputs are finite; a program needn't handle non-finite values.
Results may differ from the reference program's by a relative error of at most 0.012.
The reference program's roundings to bfloat16 on the way count: a program that leaves them out, or rounds other values in their place, can miss the bound.
Values may be sent and summed in bfloat16 or wider, within the bound.
A program may use at most 128 MiB of HBM per device.

```python
import math
import jax
import jax.numpy as jnp
from jax import lax

D = 3584
H = 16
KVH = 8
HD = 256
FF = 14336
REQ_DEV = 12
STEPS = 4
R = 48
POOL = 4096
KVW = 2048
QKVW = 8192


def layout(key):
    group_total = R // REQ_DEV
    dealing = jax.random.permutation(jax.random.fold_in(key, 11), R).astype(jnp.int32)
    longest = POOL // 2
    rest = POOL - longest
    chosen = jax.random.randint(jax.random.fold_in(key, 13), (group_total, 1), 0, REQ_DEV, dtype=jnp.int32)
    slots = jnp.arange(REQ_DEV, dtype=jnp.int32)[None, :]
    is_long = (slots == chosen).astype(jnp.int32)
    is_filler = (slots == (chosen + 1) % REQ_DEV).astype(jnp.int32)
    weights = jax.random.randint(jax.random.fold_in(key, 12), (group_total, REQ_DEV), 1, 17, dtype=jnp.int32) * (1 - is_long)
    shares = weights * rest // jnp.sum(weights, axis=1, keepdims=True)
    shares = shares + is_filler * (rest - jnp.sum(shares, axis=1, keepdims=True)) + is_long * longest
    bounds = jnp.cumsum(shares, axis=1)
    tokens = jnp.arange(POOL, dtype=jnp.int32)
    owners = jnp.sum((tokens[None, None, :] >= bounds[:, :, None]).astype(jnp.int32), axis=1).astype(jnp.int32)
    lengths = jnp.zeros((R,), jnp.int32).at[dealing].set(shares.reshape(-1).astype(jnp.int32))
    return (dealing, lengths, owners)


def draw_dealing(key, part):
    return layout(key)[0]


def draw_lengths(key, part):
    return layout(key)[1]


def draw_token_owner(key, part):
    return layout(key)[2]


def draw_project_weight(key, part):
    head_order = jax.random.permutation(jax.random.fold_in(key, 21), H).astype(jnp.float32)
    head_scale = 3.0 * jnp.exp(head_order * (jnp.log(20.0) / (H - 1)))
    query_scale = jnp.repeat(head_scale, HD)
    column_scale = jnp.concatenate([query_scale, jnp.ones((2 * KVH * HD,), jnp.float32)])
    base_key = jax.random.fold_in(key, 22)
    base = jnp.clip(jax.random.normal(base_key, (D, QKVW), jnp.float32), -6.0, 6.0)
    return (base * D ** (-0.5) * column_scale[None, :]).astype(jnp.bfloat16)


def block_levels(key, dims, cuts, low, largest):
    loudness, own = 1.0, jax.random.fold_in(key, 6)
    for axis_at, blocks in cuts:
        steps = jnp.exp(jax.random.uniform(jax.random.fold_in(own, axis_at), (blocks,), jnp.float32, low / len(cuts), largest / len(cuts)))
        loudness = loudness * jnp.repeat(steps, dims[axis_at] // blocks).reshape([-1 if axis == axis_at else 1 for axis in range(len(dims))])
    return loudness


def normal_values(key, shape, width, most, shards=(), kind=jnp.bfloat16):
    entries = jax.random.normal(key, shape, jnp.float32) * width
    if len(shards) > 0:
        entries = block_levels(key, shape, shards, -0.22, 0.18) * entries
    return jnp.clip(entries, min=-most, max=most).astype(kind)


def setup_inputs(seed: int = 0) -> dict:
    arg_keys = jax.random.split(jax.random.key(seed), 16)
    return {
        "embedded": normal_values(arg_keys[0], (STEPS, R, D), 1.0, 6.0, ((1, 4),)),
        "cache_keys": normal_values(arg_keys[1], (R // REQ_DEV, POOL, KVW), 1.0, 6.0, ((0, 4), (1, 8))),
        "cache_values": normal_values(arg_keys[2], (R // REQ_DEV, POOL, KVW), 1.0, 6.0, ((0, 4), (1, 8))),
        "token_owner": draw_token_owner(jax.random.fold_in(arg_keys[15], 71), 0),
        "dealing": draw_dealing(jax.random.fold_in(arg_keys[15], 71), 0),
        "lengths": draw_lengths(jax.random.fold_in(arg_keys[15], 71), 0),
        "project_weight": draw_project_weight(jax.random.fold_in(arg_keys[15], 71), 0),
        "output_weight": normal_values(arg_keys[7], (H * HD, D), (H * HD) ** -0.5, 0.09375, ((0, 8),)),
        "gate_weight": normal_values(arg_keys[8], (D, FF), D ** -0.5, 0.09375, ((1, 32),)),
        "up_weight": normal_values(arg_keys[9], (D, FF), D ** -0.5, 0.09375, ((1, 32),)),
        "down_weight": normal_values(arg_keys[10], (FF, D), FF ** -0.5, 0.046875, ((0, 32),)),
        "gain_first": jnp.clip(1.0 + 0.18 * jax.random.normal(arg_keys[11], (D,), jnp.float32), 0.1, 1.9),
        "gain_second": jnp.clip(1.0 + 0.18 * jax.random.normal(arg_keys[12], (D,), jnp.float32), 0.1, 1.9),
        "gain_third": jnp.clip(1.0 + 0.18 * jax.random.normal(arg_keys[13], (D,), jnp.float32), 0.1, 1.9),
        "gain_fourth": jnp.clip(1.0 + 0.18 * jax.random.normal(arg_keys[14], (D,), jnp.float32), 0.1, 1.9),
    }


soft_cap = 50.0
epsilon = 1e-06

def rms_scale(values, gain):
    mean_square = lax.optimization_barrier(jnp.mean(values * values, axis=-1, keepdims=True))
    return values * lax.rsqrt(mean_square + epsilon) * gain

def rotate(values, positions):
    half_width = values.shape[-1] // 2
    freq_index = jnp.arange(half_width, dtype=jnp.float32)
    inverse = jnp.exp(freq_index * (-2.0 * math.log(10000.0) / values.shape[-1]))
    angles = positions[:, None] * inverse[None, :]
    cosine = jnp.cos(angles)[:, None, :]
    sine = jnp.sin(angles)[:, None, :]
    first_half = values[..., :half_width]
    second_half = values[..., half_width:]
    return jnp.concatenate([first_half * cosine - second_half * sine, second_half * cosine + first_half * sine], axis=-1)

def capped_weight(scores):
    return jnp.exp(soft_cap * jnp.tanh(scores / soft_cap))

def rounded(values):
    return lax.optimization_barrier(values.astype(jnp.bfloat16)).astype(jnp.float32)

def add_fresh(totals, outputs, queries, fresh_keys, fresh_values):
    for key_rows, value_rows in zip(fresh_keys, fresh_values):
        scores = lax.optimization_barrier(jnp.sum(queries.astype(jnp.float32) * key_rows.astype(jnp.float32)[:, :, None, :], axis=-1))
        weights = capped_weight(scores)
        totals = totals + weights
        outputs = outputs + rounded(weights)[..., None] * value_rows.astype(jnp.float32)[:, :, None, :]
    return (totals, outputs)

def cache_part(queries, key_pool, value_pool, owner_row):
    scores = jnp.einsum('igqd,tgd->igqt', queries.astype(jnp.float32), key_pool.astype(jnp.float32))
    owned_mask = owner_row[None, :] == jnp.arange(queries.shape[0], dtype=jnp.int32)[:, None]
    weights = jnp.where(owned_mask[:, None, None, :], capped_weight(scores), 0.0)
    totals = lax.optimization_barrier(jnp.sum(weights, axis=-1))
    outputs = jnp.einsum('igqt,tgd->igqd', rounded(weights), value_pool.astype(jnp.float32))
    return (totals, outputs)

def reference(embedded, cache_keys, cache_values, token_owner, dealing, lengths, project_weight, output_weight, gate_weight, up_weight, down_weight, gain_first, gain_second, gain_third, gain_fourth):
    groups = R // REQ_DEV
    group_size = H // KVH
    attention_width = H * HD
    base_positions = lengths[dealing]
    key_pools = cache_keys.reshape(groups, POOL, KVH, HD)
    value_pools = cache_values.reshape(groups, POOL, KVH, HD)
    fresh_keys = []
    fresh_values = []
    results = []
    for moment in range(STEPS):
        stream = embedded[moment].astype(jnp.float32)
        normed = rms_scale(stream, gain_first).astype(jnp.bfloat16)
        projected = jnp.dot(normed, project_weight, preferred_element_type=jnp.float32).astype(jnp.bfloat16)
        positions = (base_positions + moment).astype(jnp.float32)
        query_rows = projected[:, :attention_width].astype(jnp.float32).reshape(R, H, HD)
        queries = (rotate(query_rows, positions) * HD ** (-0.5)).astype(jnp.bfloat16)
        key_rows = projected[:, attention_width:attention_width + KVW].astype(jnp.float32).reshape(R, KVH, HD)
        fresh_keys.append(rotate(key_rows, positions).astype(jnp.bfloat16))
        fresh_values.append(projected[:, attention_width + KVW:].reshape(R, KVH, HD))
        grouped = queries.reshape(groups, REQ_DEV, KVH, group_size, HD)
        totals, outputs = lax.map(lambda operands: cache_part(*operands), (grouped, key_pools, value_pools, token_owner))
        totals = totals.reshape(R, KVH, group_size)
        outputs = outputs.reshape(R, KVH, group_size, HD)
        totals, outputs = add_fresh(totals, outputs, queries.reshape(R, KVH, group_size, HD), fresh_keys, fresh_values)
        attended = (outputs / totals[..., None]).reshape(R, attention_width).astype(jnp.bfloat16)
        mixed = jnp.dot(attended, output_weight, preferred_element_type=jnp.float32)
        middle = stream + rms_scale(mixed, gain_second)
        feed_input = rms_scale(middle, gain_third).astype(jnp.bfloat16)
        gate_part = jnp.dot(feed_input, gate_weight, preferred_element_type=jnp.float32)
        up_part = jnp.dot(feed_input, up_weight, preferred_element_type=jnp.float32)
        hidden = (jax.nn.gelu(gate_part, approximate=True) * up_part).astype(jnp.bfloat16)
        summed = jnp.dot(hidden, down_weight, preferred_element_type=jnp.float32)
        results.append((middle + rms_scale(summed, gain_fourth)).astype(jnp.bfloat16))
    return jnp.stack(results)
```

```python
import math

import jax
import jax.numpy as jnp
from jax import lax
from jax.sharding import PartitionSpec as P

H = 16
KVH = 8
HD = 256
STEPS = 4


soft_cap = 50.0
epsilon = 1e-06


def rms_scale(values, gain):
    mean_square = jnp.mean(values * values, axis=-1, keepdims=True)
    return values * lax.rsqrt(mean_square + epsilon) * gain


def rotate(values, positions):
    half_width = values.shape[-1] // 2
    freq_index = jnp.arange(half_width, dtype=jnp.float32)
    inverse = jnp.exp(freq_index * (-2.0 * math.log(10000.0) / values.shape[-1]))
    angles = positions[:, None] * inverse[None, :]
    cosine = jnp.cos(angles)[:, None, :]
    sine = jnp.sin(angles)[:, None, :]
    first_half = values[..., :half_width]
    second_half = values[..., half_width:]
    return jnp.concatenate(
        [first_half * cosine - second_half * sine, second_half * cosine + first_half * sine],
        axis=-1,
    )


def capped_weight(scores):
    return jnp.exp(soft_cap * jnp.tanh(scores / soft_cap))


def rounded(values):
    return lax.optimization_barrier(values.astype(jnp.bfloat16)).astype(jnp.float32)


def body(
    embedded,
    cache_keys,
    cache_values,
    token_owner,
    dealing,
    lengths,
    project_weight,
    output_weight,
    gate_weight,
    up_weight,
    down_weight,
    gain_first,
    gain_second,
    gain_third,
    gain_fourth,
):
    row_count = embedded.shape[1]
    rows = STEPS * row_count
    width = embedded.shape[2]
    local_tokens = cache_keys.shape[1]
    value_width = cache_keys.shape[2]
    group_size = H // KVH
    attention_width = H * HD
    column_count = output_weight.shape[0]
    group_index = lax.axis_index("req")
    seq_index = lax.axis_index("seq")
    seq_size = lax.axis_size("seq")
    req_size = lax.axis_size("req")
    column_start = seq_index * column_count
    slot_requests = lax.dynamic_slice_in_dim(dealing, group_index * row_count, row_count)
    matches = slot_requests[:, None] == jnp.arange(dealing.shape[0], dtype=jnp.int32)[None, :]
    base_positions = jnp.sum(jnp.where(matches, lengths[None, :], 0), axis=1)
    positions = base_positions[None, :] + jnp.arange(STEPS, dtype=jnp.int32)[:, None]
    positions = positions.reshape(rows).astype(jnp.float32)
    key_pool = cache_keys[0].reshape(local_tokens, KVH, HD)
    value_pool = cache_values[0].reshape(local_tokens, KVH, HD)
    slots = jnp.tile(jnp.arange(row_count, dtype=jnp.int32), STEPS)
    moments = jnp.repeat(jnp.arange(STEPS, dtype=jnp.int32), row_count)
    owned_mask = token_owner[0][None, :] == slots[:, None]
    stream = embedded.reshape(rows, width).astype(jnp.float32)
    normed = rms_scale(stream, gain_first).astype(jnp.bfloat16)
    local_part = jnp.dot(normed, project_weight, preferred_element_type=jnp.float32).astype(
        jnp.bfloat16
    )
    projected = lax.all_gather(local_part, "seq", axis=1, tiled=True)
    query_rows = projected[:, :attention_width].astype(jnp.float32).reshape(rows, H, HD)
    queries = (rotate(query_rows, positions) * HD ** (-0.5)).astype(jnp.bfloat16)
    key_rows = (
        projected[:, attention_width : attention_width + value_width]
        .astype(jnp.float32)
        .reshape(rows, KVH, HD)
    )
    fresh_keys = rotate(key_rows, positions).astype(jnp.bfloat16)
    fresh_values = projected[:, attention_width + value_width :].reshape(rows, KVH, HD)
    grouped = queries.reshape(rows, KVH, group_size, HD)
    all_keys = jnp.concatenate([key_pool, fresh_keys], axis=0)
    all_values = jnp.concatenate([value_pool, fresh_values], axis=0)
    fresh_mask = (
        (slots[None, :] == slots[:, None])
        & (moments[None, :] <= moments[:, None])
        & (seq_index == 0)
    )
    mask = jnp.concatenate([owned_mask, fresh_mask], axis=1)
    scores = jnp.einsum("igqd,tgd->igqt", grouped, all_keys, preferred_element_type=jnp.float32)
    weights = jnp.where(mask[:, None, None, :], capped_weight(scores), 0.0)
    totals = lax.psum(jnp.sum(weights, axis=-1), "seq").reshape(rows, H)
    outputs = jnp.einsum(
        "igqt,tgd->igqd",
        weights.astype(jnp.bfloat16),
        all_values,
        preferred_element_type=jnp.float32,
    ).reshape(rows, attention_width)
    outputs = lax.psum_scatter(outputs, "seq", scatter_dimension=1, tiled=True)
    spread = jnp.repeat(totals, HD, axis=1)
    spread = lax.dynamic_slice_in_dim(spread, column_start, column_count, 1)
    attended = (outputs / spread).astype(jnp.bfloat16)
    partial = jnp.dot(attended, output_weight, preferred_element_type=jnp.float32)
    mixed = lax.psum(partial, "seq")
    middle = stream + rms_scale(mixed, gain_second)
    feed_input = rms_scale(middle, gain_third).astype(jnp.bfloat16)
    block_rows = lax.all_gather(feed_input, "req", axis=0, tiled=True)
    gate_part = jnp.dot(block_rows, gate_weight, preferred_element_type=jnp.float32)
    up_part = jnp.dot(block_rows, up_weight, preferred_element_type=jnp.float32)
    hidden = (jax.nn.gelu(gate_part, approximate=True) * up_part).astype(jnp.bfloat16)
    summed = jnp.dot(hidden, down_weight, preferred_element_type=jnp.float32)
    summed = lax.psum_scatter(summed, "req", scatter_dimension=0, tiled=True)
    summed = lax.psum(summed, "seq")
    results = (middle + rms_scale(summed, gain_fourth)).astype(jnp.bfloat16)
    return results.reshape(STEPS, row_count, width)


def solution(mesh):
    return jax.shard_map(
        body,
        mesh=mesh,
        in_specs=(
            P(None, "req", None),
            P("req", "seq", None),
            P("req", "seq", None),
            P("req", "seq"),
            P(),
            P(),
            P(None, "seq"),
            P("seq", None),
            P(None, ("req", "seq")),
            P(None, ("req", "seq")),
            P(("req", "seq"), None),
            P(),
            P(),
            P(),
            P(),
        ),
        out_specs=P(None, "req", None),
        check_vma=False,
    )
```

```python
import math

import jax
import jax.numpy as jnp
from jax import lax
from jax.experimental import pallas as pl
from jax.experimental.pallas import tpu as pltpu
from jax.sharding import PartitionSpec as P

H = 16
KVH = 8
HD = 256
STEPS = 4


soft_cap = 50.0
epsilon = 1e-06


def rms_scale(values, gain):
    mean_square = jnp.mean(values * values, axis=-1, keepdims=True)
    return values * lax.rsqrt(mean_square + epsilon) * gain


def rotate(values, positions):
    half_width = values.shape[-1] // 2
    freq_index = jnp.arange(half_width, dtype=jnp.float32)
    inverse = jnp.exp(freq_index * (-2.0 * math.log(10000.0) / values.shape[-1]))
    angles = positions[:, None] * inverse[None, :]
    cosine = jnp.cos(angles)[:, None, :]
    sine = jnp.sin(angles)[:, None, :]
    first_half = values[..., :half_width]
    second_half = values[..., half_width:]
    return jnp.concatenate(
        [first_half * cosine - second_half * sine, second_half * cosine + first_half * sine],
        axis=-1,
    )


def capped_weight(scores):
    return jnp.exp(soft_cap * jnp.tanh(scores / soft_cap))


def rounded(values):
    return lax.optimization_barrier(values.astype(jnp.bfloat16)).astype(jnp.float32)


def plain_body(
    embedded,
    cache_keys,
    cache_values,
    token_owner,
    dealing,
    lengths,
    project_weight,
    output_weight,
    gate_weight,
    up_weight,
    down_weight,
    gain_first,
    gain_second,
    gain_third,
    gain_fourth,
):
    row_count = embedded.shape[1]
    rows = STEPS * row_count
    width = embedded.shape[2]
    local_tokens = cache_keys.shape[1]
    value_width = cache_keys.shape[2]
    group_size = H // KVH
    attention_width = H * HD
    column_count = output_weight.shape[0]
    group_index = lax.axis_index("req")
    seq_index = lax.axis_index("seq")
    seq_size = lax.axis_size("seq")
    req_size = lax.axis_size("req")
    column_start = seq_index * column_count
    slot_requests = lax.dynamic_slice_in_dim(dealing, group_index * row_count, row_count)
    matches = slot_requests[:, None] == jnp.arange(dealing.shape[0], dtype=jnp.int32)[None, :]
    base_positions = jnp.sum(jnp.where(matches, lengths[None, :], 0), axis=1)
    positions = base_positions[None, :] + jnp.arange(STEPS, dtype=jnp.int32)[:, None]
    positions = positions.reshape(rows).astype(jnp.float32)
    key_pool = cache_keys[0].reshape(local_tokens, KVH, HD)
    value_pool = cache_values[0].reshape(local_tokens, KVH, HD)
    slots = jnp.tile(jnp.arange(row_count, dtype=jnp.int32), STEPS)
    moments = jnp.repeat(jnp.arange(STEPS, dtype=jnp.int32), row_count)
    owned_mask = token_owner[0][None, :] == slots[:, None]
    stream = embedded.reshape(rows, width).astype(jnp.float32)
    normed = rms_scale(stream, gain_first).astype(jnp.bfloat16)
    local_part = jnp.dot(normed, project_weight, preferred_element_type=jnp.float32).astype(
        jnp.bfloat16
    )
    projected = lax.all_gather(local_part, "seq", axis=1, tiled=True)
    query_rows = projected[:, :attention_width].astype(jnp.float32).reshape(rows, H, HD)
    queries = (rotate(query_rows, positions) * HD ** (-0.5)).astype(jnp.bfloat16)
    key_rows = (
        projected[:, attention_width : attention_width + value_width]
        .astype(jnp.float32)
        .reshape(rows, KVH, HD)
    )
    fresh_keys = rotate(key_rows, positions).astype(jnp.bfloat16)
    fresh_values = projected[:, attention_width + value_width :].reshape(rows, KVH, HD)
    grouped = queries.reshape(rows, KVH, group_size, HD)
    all_keys = jnp.concatenate([key_pool, fresh_keys], axis=0)
    all_values = jnp.concatenate([value_pool, fresh_values], axis=0)
    fresh_mask = (
        (slots[None, :] == slots[:, None])
        & (moments[None, :] <= moments[:, None])
        & (seq_index == 0)
    )
    mask = jnp.concatenate([owned_mask, fresh_mask], axis=1)
    scores = jnp.einsum("igqd,tgd->igqt", grouped, all_keys, preferred_element_type=jnp.float32)
    weights = jnp.where(mask[:, None, None, :], capped_weight(scores), 0.0)
    totals = lax.psum(jnp.sum(weights, axis=-1), "seq").reshape(rows, H)
    outputs = jnp.einsum(
        "igqt,tgd->igqd",
        weights.astype(jnp.bfloat16),
        all_values,
        preferred_element_type=jnp.float32,
    ).reshape(rows, attention_width)
    outputs = lax.psum_scatter(outputs, "seq", scatter_dimension=1, tiled=True)
    spread = jnp.repeat(totals, HD, axis=1)
    spread = lax.dynamic_slice_in_dim(spread, column_start, column_count, 1)
    attended = (outputs / spread).astype(jnp.bfloat16)
    partial = jnp.dot(attended, output_weight, preferred_element_type=jnp.float32)
    mixed = lax.psum(partial, "seq")
    middle = stream + rms_scale(mixed, gain_second)
    feed_input = rms_scale(middle, gain_third).astype(jnp.bfloat16)
    block_rows = lax.all_gather(feed_input, "req", axis=0, tiled=True)
    gate_part = jnp.dot(block_rows, gate_weight, preferred_element_type=jnp.float32)
    up_part = jnp.dot(block_rows, up_weight, preferred_element_type=jnp.float32)
    hidden = (jax.nn.gelu(gate_part, approximate=True) * up_part).astype(jnp.bfloat16)
    summed = jnp.dot(hidden, down_weight, preferred_element_type=jnp.float32)
    summed = lax.psum_scatter(summed, "req", scatter_dimension=0, tiled=True)
    summed = lax.psum(summed, "seq")
    results = (middle + rms_scale(summed, gain_fourth)).astype(jnp.bfloat16)
    return results.reshape(STEPS, row_count, width)


MESH = pl.DeviceIdType.MESH
SEQ = 8
REQ = 4
OWNERS = 6
TILE = 8
MIX_CHUNKS = 2
SUM_CHUNKS = 4


def kernel(
    x_ref, cos_ref, sin_ref, mask_ref, fresh_mask_ref, g1_ref, g2_ref, g3_ref, g4_ref,
    pw_hbm, ck_hbm, cv_hbm, ow_hbm, gw_hbm, uw_hbm, dw_hbm,
    out_ref,
    pw, ck, cv, ow, gw, uw, dw,
    gbuf, bsend, brecv, tot_ref, tsend, trecv, csend, crecv, mid_ref, feed, lhs_ref, hid_ref,
    part_ref, e1send, e1recv, e2send, e2recv, e3send, e3recv,
    load_sem, a_send, a_recv, b_send, b_recv, t_send, t_recv, c_send, c_recv,
    d_send, d_recv, d2_send, d2_recv, e1_ssem, e1_rsem, e2_ssem, e2_rsem, e3_ssem, e3_rsem,
    f_send, f_recv,
):
    me = lax.axis_index("seq")
    row = lax.axis_index("req")
    width = x_ref.shape[2]
    rows = OWNERS * TILE
    ff = gw.shape[1]
    other_core = row + 1 - 2 * lax.rem(row, 2)
    other_y = lax.rem(row + 2, REQ)
    is_owner = (me >= 1) & (me <= OWNERS)
    mine = jnp.minimum(jnp.maximum(me - 1, 0), OWNERS - 1)

    loads = [
        pltpu.make_async_copy(src, dst, load_sem.at[n])
        for n, (src, dst) in enumerate(
            [(pw_hbm, pw), (ck_hbm, ck), (cv_hbm, cv), (ow_hbm, ow), (gw_hbm, gw), (uw_hbm, uw)]
        )
    ]
    dw[ff:, :] = jnp.zeros((dw.shape[0] - ff, width), dw.dtype)
    hid_ref[...] = jnp.zeros_like(hid_ref)
    loads.append(pltpu.make_async_copy(dw_hbm, dw.at[pl.ds(0, ff)], load_sem.at[6]))
    for load in loads:
        load.start()

    barrier = pltpu.get_barrier_semaphore()
    for d in range(1, SEQ):
        pl.semaphore_signal(
            barrier, inc=1, device_id={"seq": lax.rem(me + d, SEQ)}, device_id_type=MESH
        )
    pl.semaphore_signal(barrier, inc=1, device_id={"req": other_core}, device_id_type=MESH)
    pl.semaphore_signal(barrier, inc=1, device_id={"req": other_y}, device_id_type=MESH)

    def remote(src, dst, send, recv, target):
        return pltpu.make_async_remote_copy(
            src_ref=src, dst_ref=dst, send_sem=send, recv_sem=recv,
            device_id=target, device_id_type=MESH,
        )

    def rms(values, gain):
        mean_square = jnp.mean(values * values, axis=-1, keepdims=True)
        return values * lax.rsqrt(mean_square + epsilon) * gain

    stream = x_ref[...].astype(jnp.float32).reshape(rows, width)
    normed = rms(stream, g1_ref[...]).astype(jnp.bfloat16)
    loads[0].wait()
    projected = jnp.dot(normed, pw[...], preferred_element_type=jnp.float32)
    projected = projected.astype(jnp.bfloat16).astype(jnp.float32)
    cosine, sine = cos_ref[...], sin_ref[...]
    half = HD // 2
    for h in range(pw.shape[1] // HD):
        a = projected[:, h * HD : h * HD + half]
        b = projected[:, h * HD + half : (h + 1) * HD]
        gbuf[me, :, h * HD : h * HD + half] = (a * cosine - b * sine).astype(jnp.bfloat16)
        gbuf[me, :, h * HD + half : (h + 1) * HD] = (b * cosine + a * sine).astype(jnp.bfloat16)
    pl.semaphore_wait(barrier, SEQ + 1)

    def a_copy(d):
        return remote(
            gbuf.at[me], gbuf.at[me], a_send.at[d - 1], a_recv.at[me],
            {"seq": lax.rem(me + d, SEQ)},
        )

    for d in range(1, SEQ):
        a_copy(d).start()
    for d in range(1, SEQ):
        source = lax.rem(me + d, SEQ)
        remote(
            gbuf.at[source], gbuf.at[source], a_send.at[d - 1], a_recv.at[source], {"seq": source}
        ).wait_recv()

    loads[1].wait()
    loads[2].wait()
    owned = mask_ref[...] > 0.5
    lanes = lax.broadcasted_iota(jnp.int32, (2 * rows, 128), 1)
    totals = jnp.zeros((2 * rows, 128), jnp.float32)

    def attend(queries, keys, values, allowed):
        scores = lax.dot_general(
            queries, keys, (((1,), (1,)), ((), ())), preferred_element_type=jnp.float32
        )
        weights = jnp.where(allowed, capped_weight(scores), 0.0)
        outputs = jnp.dot(
            weights.astype(jnp.bfloat16), values, preferred_element_type=jnp.float32
        )
        return jnp.sum(weights, axis=-1, keepdims=True), outputs

    def b_copy(j):
        return remote(
            bsend.at[j - 1], brecv.at[j - 1], b_send.at[j - 1], b_recv.at[j - 1],
            {"seq": lax.rem(me + j, SEQ)},
        )

    def t_copy(j):
        return remote(
            tsend, trecv.at[j - 1], t_send.at[j - 1], t_recv.at[j - 1],
            {"seq": lax.rem(me + j, SEQ)},
        )

    for j in range(1, SEQ + 1):
        e = lax.rem(me + j, SEQ)
        block = e // 2
        first = pl.multiple_of(lax.rem(e, 2) * (2 * HD), 2 * HD)
        queries = jnp.concatenate(
            [gbuf[block, :, pl.ds(first, HD)], gbuf[block, :, pl.ds(first + HD, HD)]], axis=0
        )
        head = pl.ds(pl.multiple_of(e * HD, HD), HD)
        total, outputs = attend(queries, ck[:, head], cv[:, head], owned)
        if j < SEQ:
            bsend[j - 1] = outputs.astype(jnp.bfloat16)
            b_copy(j).start()
        else:
            fresh = pl.ds(pl.multiple_of(lax.rem(e, 4) * HD, HD), HD)
            fresh_total, fresh_outputs = attend(
                queries, gbuf[4 + e // 4, :, fresh], gbuf[6 + e // 4, :, fresh],
                fresh_mask_ref[...] > 0.5,
            )
            total = total + fresh_total
            outputs = outputs + fresh_outputs
        totals = totals + jnp.where(lanes == e, total, 0.0)
    tot_ref[2 * rows :, :] = jnp.zeros((128 - 2 * rows, 128), jnp.float32)
    tot_ref[: 2 * rows, :] = totals
    tsend[...] = tot_ref[...].T[:KVH]
    for j in range(1, SEQ):
        t_copy(j).start()
    everyone = tsend[...]
    for j in range(1, SEQ):
        b_copy(j).wait_recv()
        t_copy(j).wait_recv()
        outputs = outputs + brecv[j - 1].astype(jnp.float32)
        everyone = everyone + trecv[j - 1]
    tot_ref[...] = jnp.zeros((128, 128), jnp.float32)
    tot_ref[:KVH, :] = everyone
    spread = tot_ref[...].T
    column = jnp.sum(jnp.where(lanes == me, spread[: 2 * rows], 0.0), axis=-1, keepdims=True)
    attended = outputs / column
    attended = jnp.concatenate([attended[:rows], attended[rows:]], axis=1).astype(jnp.bfloat16)

    loads[3].wait()
    mix = width // MIX_CHUNKS

    def c_send_to(c, d):
        target = lax.rem(me + d, SEQ)
        owner = jnp.minimum(jnp.maximum(target - 1, 0), OWNERS - 1)
        copy = remote(
            csend.at[c, owner], crecv.at[c, d - 1], c_send.at[c, d - 1], c_recv.at[c, d - 1],
            {"seq": target},
        )
        return (target >= 1) & (target <= OWNERS), copy

    for c in range(MIX_CHUNKS):
        part = jnp.dot(
            attended, ow[:, c * mix : (c + 1) * mix], preferred_element_type=jnp.float32
        )
        csend[c] = part.reshape(OWNERS, TILE, mix).astype(jnp.bfloat16)
        for d in range(1, SEQ):
            pred, copy = c_send_to(c, d)
            pl.when(pred)(copy.start)

    def d_copy(d):
        return remote(
            feed.at[0, mine], feed.at[0, mine], d_send.at[d - 1], d_recv.at[mine],
            {"seq": lax.rem(me + d, SEQ)},
        )

    @pl.when(is_owner)
    def _():
        pieces = []
        for c in range(MIX_CHUNKS):
            piece = csend[c, mine].astype(jnp.float32)
            for d in range(1, SEQ):
                c_send_to(c, d)[1].wait_recv()
                piece = piece + crecv[c, d - 1].astype(jnp.float32)
            pieces.append(piece)
        mixed = jnp.concatenate(pieces, axis=1)
        middle = x_ref[mine].astype(jnp.float32) + rms(mixed, g2_ref[...])
        mid_ref[...] = middle
        feed[0, mine] = rms(middle, g3_ref[...]).astype(jnp.bfloat16)
        for d in range(1, SEQ):
            d_copy(d).start()

    def to_y(o):
        return remote(
            feed.at[0, o], feed.at[2, o], d2_send.at[0, o], d2_recv.at[0, o], {"req": other_y}
        )

    def to_core(o):
        return remote(
            feed.at[0, o], feed.at[1, o], d2_send.at[1, o], d2_recv.at[1, o], {"req": other_core}
        )

    def to_corner(o):
        return remote(
            feed.at[2, o], feed.at[3, o], d2_send.at[2, o], d2_recv.at[2, o], {"req": other_core}
        )

    for o in range(OWNERS):
        @pl.when(me != o + 1)
        def _():
            remote(
                feed.at[0, o], feed.at[0, o], d_send.at[0], d_recv.at[o], {"seq": o + 1}
            ).wait_recv()

        to_y(o).start()
        to_core(o).start()
    for o in range(OWNERS):
        to_y(o).wait_recv()
        to_corner(o).start()
    for o in range(OWNERS):
        to_core(o).wait_recv()
        to_corner(o).wait_recv()

    for q in range(REQ):
        lhs_ref[q * rows : (q + 1) * rows, :] = (
            feed[q].astype(jnp.float32).reshape(rows, width).astype(jnp.bfloat16)
        )
    loads[4].wait()
    loads[5].wait()
    gate_part = jnp.dot(lhs_ref[...], gw[...], preferred_element_type=jnp.float32)
    up_part = jnp.dot(lhs_ref[...], uw[...], preferred_element_type=jnp.float32)
    hidden = (jax.nn.gelu(gate_part, approximate=True) * up_part).astype(jnp.bfloat16)
    hid_ref[:, :ff] = hidden
    loads[6].wait()
    piece_width = width // SUM_CHUNKS

    def e1_copy(c):
        return remote(
            e1send.at[c], e1recv.at[c], e1_ssem.at[c], e1_rsem.at[c], {"req": other_core}
        )

    def e2_copy(c):
        return remote(e2send.at[c], e2recv.at[c], e2_ssem.at[c], e2_rsem.at[c], {"req": other_y})

    def e3_copy(c, d):
        target = lax.rem(me + d, SEQ)
        owner = jnp.minimum(jnp.maximum(target - 1, 0), OWNERS - 1)
        copy = remote(
            e3send.at[c, owner], e3recv.at[c, d - 1], e3_ssem.at[c, d - 1], e3_rsem.at[c, d - 1],
            {"seq": target},
        )
        return (target >= 1) & (target <= OWNERS), copy

    for c in range(SUM_CHUNKS):
        part = jnp.dot(
            hid_ref[...],
            dw[:, c * piece_width : (c + 1) * piece_width],
            preferred_element_type=jnp.float32,
        )
        e1send[c, :rows] = part[rows : 2 * rows].astype(jnp.bfloat16)
        e1send[c, rows:] = part[3 * rows :].astype(jnp.bfloat16)
        part_ref[c, :rows] = part[:rows]
        part_ref[c, rows:] = part[2 * rows : 3 * rows]
        e1_copy(c).start()
    for c in range(SUM_CHUNKS):
        e1_copy(c).wait_recv()
        e2send[c] = (part_ref[c, rows:] + e1recv[c, rows:].astype(jnp.float32)).astype(
            jnp.bfloat16
        )
        e2_copy(c).start()
    for c in range(SUM_CHUNKS):
        e2_copy(c).wait_recv()
        kept = part_ref[c, :rows] + e1recv[c, :rows].astype(jnp.float32)
        kept = kept + e2recv[c].astype(jnp.float32)
        e3send[c] = kept.reshape(OWNERS, TILE, piece_width).astype(jnp.bfloat16)
        for d in range(1, SEQ):
            pred, copy = e3_copy(c, d)
            pl.when(pred)(copy.start)

    def f_copy(d):
        return remote(
            out_ref.at[mine], out_ref.at[mine], f_send.at[d - 1], f_recv.at[mine],
            {"seq": lax.rem(me + d, SEQ)},
        )

    @pl.when(is_owner)
    def _():
        pieces = []
        for c in range(SUM_CHUNKS):
            piece = e3send[c, mine].astype(jnp.float32)
            for d in range(1, SEQ):
                e3_copy(c, d)[1].wait_recv()
                piece = piece + e3recv[c, d - 1].astype(jnp.float32)
            pieces.append(piece)
        summed = jnp.concatenate(pieces, axis=1)
        out_ref[mine] = (mid_ref[...] + rms(summed, g4_ref[...])).astype(jnp.bfloat16)
        for d in range(1, SEQ):
            f_copy(d).start()

    for o in range(OWNERS):
        @pl.when(me != o + 1)
        def _():
            remote(
                out_ref.at[o], out_ref.at[o], f_send.at[0], f_recv.at[o], {"seq": o + 1}
            ).wait_recv()

    for d in range(1, SEQ):
        a_copy(d).wait_send()
        b_copy(d).wait_send()
        t_copy(d).wait_send()
        for c in range(MIX_CHUNKS):
            pred, copy = c_send_to(c, d)
            pl.when(pred)(copy.wait_send)
        for c in range(SUM_CHUNKS):
            pred, copy = e3_copy(c, d)
            pl.when(pred)(copy.wait_send)
    for o in range(OWNERS):
        to_y(o).wait_send()
        to_core(o).wait_send()
        to_corner(o).wait_send()
    for c in range(SUM_CHUNKS):
        e1_copy(c).wait_send()
        e2_copy(c).wait_send()

    @pl.when(is_owner)
    def _():
        for d in range(1, SEQ):
            d_copy(d).wait_send()
            f_copy(d).wait_send()


def fused_body(
    embedded,
    cache_keys,
    cache_values,
    token_owner,
    dealing,
    lengths,
    project_weight,
    output_weight,
    gate_weight,
    up_weight,
    down_weight,
    gain_first,
    gain_second,
    gain_third,
    gain_fourth,
):
    row_count = embedded.shape[1]
    rows = STEPS * row_count
    width = embedded.shape[2]
    tokens = cache_keys.shape[1]
    kvw = cache_keys.shape[2]
    columns = project_weight.shape[1]
    depth = output_weight.shape[0]
    ff = gate_weight.shape[1]
    ff_pad = -(-ff // 128) * 128
    mix = width // MIX_CHUNKS
    piece = width // SUM_CHUNKS
    group_index = lax.axis_index("req")
    seq_index = lax.axis_index("seq")
    slot_requests = lax.dynamic_slice_in_dim(dealing, group_index * row_count, row_count)
    matches = slot_requests[:, None] == jnp.arange(dealing.shape[0], dtype=jnp.int32)[None, :]
    base_positions = jnp.sum(jnp.where(matches, lengths[None, :], 0), axis=1)
    positions = base_positions[None, :] + jnp.arange(STEPS, dtype=jnp.int32)[:, None]
    positions = positions.reshape(rows).astype(jnp.float32)
    freq_index = jnp.arange(HD // 2, dtype=jnp.float32)
    inverse = jnp.exp(freq_index * (-2.0 * math.log(10000.0) / HD))
    angles = positions[:, None] * inverse[None, :]
    scale = jnp.where(seq_index < SEQ // 2, HD ** (-0.5), 1.0)
    turned = seq_index < 3 * SEQ // 4
    cosine = jnp.where(turned, jnp.cos(angles) * scale, 1.0)
    sine = jnp.where(turned, jnp.sin(angles) * scale, 0.0)
    slots = jnp.tile(jnp.arange(row_count, dtype=jnp.int32), STEPS)
    moments = jnp.repeat(jnp.arange(STEPS, dtype=jnp.int32), row_count)
    mask = (token_owner[0][None, :] == jnp.tile(slots, 2)[:, None]).astype(jnp.float32)
    fresh_mask = (slots[None, :] == slots[:, None]) & (moments[None, :] <= moments[:, None])
    fresh_mask = jnp.tile(fresh_mask, (2, 1)).astype(jnp.float32)
    bf16, f32 = jnp.bfloat16, jnp.float32
    dma = pltpu.SemaphoreType.DMA
    vmem = pl.BlockSpec(memory_space=pltpu.VMEM)
    hbm = pl.BlockSpec(memory_space=pl.ANY)
    out = pl.pallas_call(
        kernel,
        out_shape=jax.ShapeDtypeStruct((OWNERS, TILE, width), bf16),
        in_specs=[vmem] * 9 + [hbm] * 7,
        out_specs=vmem,
        scratch_shapes=[
            pltpu.VMEM((width, columns), bf16),
            pltpu.VMEM((tokens, kvw), bf16),
            pltpu.VMEM((tokens, kvw), bf16),
            pltpu.VMEM((depth, width), bf16),
            pltpu.VMEM((width, ff), bf16),
            pltpu.VMEM((width, ff), bf16),
            pltpu.VMEM((ff_pad, width), bf16),
            pltpu.VMEM((SEQ, rows, columns), bf16),
            pltpu.VMEM((SEQ - 1, 2 * rows, HD), bf16),
            pltpu.VMEM((SEQ - 1, 2 * rows, HD), bf16),
            pltpu.VMEM((128, 128), f32),
            pltpu.VMEM((KVH, 128), f32),
            pltpu.VMEM((SEQ - 1, KVH, 128), f32),
            pltpu.VMEM((MIX_CHUNKS, OWNERS, TILE, mix), bf16),
            pltpu.VMEM((MIX_CHUNKS, SEQ - 1, TILE, mix), bf16),
            pltpu.VMEM((TILE, width), f32),
            pltpu.VMEM((REQ, OWNERS, TILE, width), bf16),
            pltpu.VMEM((REQ * rows, width), bf16),
            pltpu.VMEM((REQ * rows, ff_pad), bf16),
            pltpu.VMEM((SUM_CHUNKS, 2 * rows, piece), f32),
            pltpu.VMEM((SUM_CHUNKS, 2 * rows, piece), bf16),
            pltpu.VMEM((SUM_CHUNKS, 2 * rows, piece), bf16),
            pltpu.VMEM((SUM_CHUNKS, rows, piece), bf16),
            pltpu.VMEM((SUM_CHUNKS, rows, piece), bf16),
            pltpu.VMEM((SUM_CHUNKS, OWNERS, TILE, piece), bf16),
            pltpu.VMEM((SUM_CHUNKS, SEQ - 1, TILE, piece), bf16),
            dma((7,)),
            dma((SEQ - 1,)),
            dma((SEQ,)),
            dma((SEQ - 1,)),
            dma((SEQ - 1,)),
            dma((SEQ - 1,)),
            dma((SEQ - 1,)),
            dma((MIX_CHUNKS, SEQ - 1)),
            dma((MIX_CHUNKS, SEQ - 1)),
            dma((SEQ - 1,)),
            dma((OWNERS,)),
            dma((3, OWNERS)),
            dma((3, OWNERS)),
            dma((SUM_CHUNKS,)),
            dma((SUM_CHUNKS,)),
            dma((SUM_CHUNKS,)),
            dma((SUM_CHUNKS,)),
            dma((SUM_CHUNKS, SEQ - 1)),
            dma((SUM_CHUNKS, SEQ - 1)),
            dma((SEQ - 1,)),
            dma((OWNERS,)),
        ],
        compiler_params=pltpu.CompilerParams(
            collective_id=0, has_side_effects=True, vmem_limit_bytes=58 << 20
        ),
    )(
        embedded.reshape(OWNERS, TILE, width),
        cosine,
        sine,
        mask,
        fresh_mask,
        gain_first[None, :],
        gain_second[None, :],
        gain_third[None, :],
        gain_fourth[None, :],
        project_weight,
        cache_keys[0],
        cache_values[0],
        output_weight,
        gate_weight,
        up_weight,
        down_weight,
    )
    return out.reshape(STEPS, row_count, width)


def body(*args):
    embedded, cache_keys = args[0], args[1]
    rows = STEPS * embedded.shape[1]
    fits = (
        lax.axis_size("seq") == SEQ
        and lax.axis_size("req") == REQ
        and rows == OWNERS * TILE
        and KVH == SEQ
        and cache_keys.shape[2] == KVH * HD
    )
    return fused_body(*args) if fits else plain_body(*args)


def solution(mesh):
    return jax.shard_map(
        body,
        mesh=mesh,
        in_specs=(
            P(None, "req", None),
            P("req", "seq", None),
            P("req", "seq", None),
            P("req", "seq"),
            P(),
            P(),
            P(None, "seq"),
            P("seq", None),
            P(None, ("req", "seq")),
            P(None, ("req", "seq")),
            P(("req", "seq"), None),
            P(),
            P(),
            P(),
            P(),
        ),
        out_specs=P(None, "req", None),
        check_vma=False,
    )
```

```python
import math

import jax
import jax.numpy as jnp
from jax import lax
from jax.experimental import pallas as pl
from jax.experimental.pallas import tpu as pltpu
from jax.sharding import PartitionSpec as P

H = 16
KVH = 8
HD = 256
STEPS = 4


soft_cap = 50.0
epsilon = 1e-06


def rms_scale(values, gain):
    mean_square = jnp.mean(values * values, axis=-1, keepdims=True)
    return values * lax.rsqrt(mean_square + epsilon) * gain


def rotate(values, positions):
    half_width = values.shape[-1] // 2
    freq_index = jnp.arange(half_width, dtype=jnp.float32)
    inverse = jnp.exp(freq_index * (-2.0 * math.log(10000.0) / values.shape[-1]))
    angles = positions[:, None] * inverse[None, :]
    cosine = jnp.cos(angles)[:, None, :]
    sine = jnp.sin(angles)[:, None, :]
    first_half = values[..., :half_width]
    second_half = values[..., half_width:]
    return jnp.concatenate(
        [first_half * cosine - second_half * sine, second_half * cosine + first_half * sine],
        axis=-1,
    )


def capped_weight(scores):
    return jnp.exp(soft_cap * jnp.tanh(scores / soft_cap))


def rounded(values):
    return lax.optimization_barrier(values.astype(jnp.bfloat16)).astype(jnp.float32)


def plain_body(
    embedded,
    cache_keys,
    cache_values,
    token_owner,
    dealing,
    lengths,
    project_weight,
    output_weight,
    gate_weight,
    up_weight,
    down_weight,
    gain_first,
    gain_second,
    gain_third,
    gain_fourth,
):
    row_count = embedded.shape[1]
    rows = STEPS * row_count
    width = embedded.shape[2]
    local_tokens = cache_keys.shape[1]
    value_width = cache_keys.shape[2]
    group_size = H // KVH
    attention_width = H * HD
    column_count = output_weight.shape[0]
    group_index = lax.axis_index("req")
    seq_index = lax.axis_index("seq")
    seq_size = lax.axis_size("seq")
    req_size = lax.axis_size("req")
    column_start = seq_index * column_count
    slot_requests = lax.dynamic_slice_in_dim(dealing, group_index * row_count, row_count)
    matches = slot_requests[:, None] == jnp.arange(dealing.shape[0], dtype=jnp.int32)[None, :]
    base_positions = jnp.sum(jnp.where(matches, lengths[None, :], 0), axis=1)
    positions = base_positions[None, :] + jnp.arange(STEPS, dtype=jnp.int32)[:, None]
    positions = positions.reshape(rows).astype(jnp.float32)
    key_pool = cache_keys[0].reshape(local_tokens, KVH, HD)
    value_pool = cache_values[0].reshape(local_tokens, KVH, HD)
    slots = jnp.tile(jnp.arange(row_count, dtype=jnp.int32), STEPS)
    moments = jnp.repeat(jnp.arange(STEPS, dtype=jnp.int32), row_count)
    owned_mask = token_owner[0][None, :] == slots[:, None]
    stream = embedded.reshape(rows, width).astype(jnp.float32)
    normed = rms_scale(stream, gain_first).astype(jnp.bfloat16)
    local_part = jnp.dot(normed, project_weight, preferred_element_type=jnp.float32).astype(
        jnp.bfloat16
    )
    projected = lax.all_gather(local_part, "seq", axis=1, tiled=True)
    query_rows = projected[:, :attention_width].astype(jnp.float32).reshape(rows, H, HD)
    queries = (rotate(query_rows, positions) * HD ** (-0.5)).astype(jnp.bfloat16)
    key_rows = (
        projected[:, attention_width : attention_width + value_width]
        .astype(jnp.float32)
        .reshape(rows, KVH, HD)
    )
    fresh_keys = rotate(key_rows, positions).astype(jnp.bfloat16)
    fresh_values = projected[:, attention_width + value_width :].reshape(rows, KVH, HD)
    grouped = queries.reshape(rows, KVH, group_size, HD)
    all_keys = jnp.concatenate([key_pool, fresh_keys], axis=0)
    all_values = jnp.concatenate([value_pool, fresh_values], axis=0)
    fresh_mask = (
        (slots[None, :] == slots[:, None])
        & (moments[None, :] <= moments[:, None])
        & (seq_index == 0)
    )
    mask = jnp.concatenate([owned_mask, fresh_mask], axis=1)
    scores = jnp.einsum("igqd,tgd->igqt", grouped, all_keys, preferred_element_type=jnp.float32)
    weights = jnp.where(mask[:, None, None, :], capped_weight(scores), 0.0)
    totals = lax.psum(jnp.sum(weights, axis=-1), "seq").reshape(rows, H)
    outputs = jnp.einsum(
        "igqt,tgd->igqd",
        weights.astype(jnp.bfloat16),
        all_values,
        preferred_element_type=jnp.float32,
    ).reshape(rows, attention_width)
    outputs = lax.psum_scatter(outputs, "seq", scatter_dimension=1, tiled=True)
    spread = jnp.repeat(totals, HD, axis=1)
    spread = lax.dynamic_slice_in_dim(spread, column_start, column_count, 1)
    attended = (outputs / spread).astype(jnp.bfloat16)
    partial = jnp.dot(attended, output_weight, preferred_element_type=jnp.float32)
    mixed = lax.psum(partial, "seq")
    middle = stream + rms_scale(mixed, gain_second)
    feed_input = rms_scale(middle, gain_third).astype(jnp.bfloat16)
    block_rows = lax.all_gather(feed_input, "req", axis=0, tiled=True)
    gate_part = jnp.dot(block_rows, gate_weight, preferred_element_type=jnp.float32)
    up_part = jnp.dot(block_rows, up_weight, preferred_element_type=jnp.float32)
    hidden = (jax.nn.gelu(gate_part, approximate=True) * up_part).astype(jnp.bfloat16)
    summed = jnp.dot(hidden, down_weight, preferred_element_type=jnp.float32)
    summed = lax.psum_scatter(summed, "req", scatter_dimension=0, tiled=True)
    summed = lax.psum(summed, "seq")
    results = (middle + rms_scale(summed, gain_fourth)).astype(jnp.bfloat16)
    return results.reshape(STEPS, row_count, width)


MESH = pl.DeviceIdType.MESH
SEQ = 8
REQ = 4
OWNERS = 6
TILE = 8
MIX_CHUNKS = 2
SUM_CHUNKS = 4


def kernel(
    x_ref, cos_ref, sin_ref, owner_ref, g1_ref, g2_ref, g3_ref, g4_ref,
    pw_hbm, ck_hbm, cv_hbm, ow_hbm, gw_hbm, uw_hbm, dw_hbm,
    out_ref,
    pw, ck, cv, ow, gw, uw, dw,
    xs_ref, res_ref, gbuf, bsend, brecv, tot_ref, tsend, trecv, csend, crecv, mid_ref, feed, lhs_ref, hid_ref,
    part_ref, e1send, e1recv, e2send, e2recv, e3send, e3recv,
    load_sem, a_send, a_recv, a_fwd, b_send, b_recv, t_send, t_recv, c_send, c_recv,
    d_send, d_recv, d_fwd, d2_send, d2_recv, e1_ssem, e1_rsem, e2_ssem, e2_rsem, e3_ssem, e3_rsem,
    f_send, f_recv, f_fwd,
):
    me = lax.axis_index("seq")
    row = lax.axis_index("req")
    width = x_ref.shape[2]
    rows = OWNERS * TILE
    ff = gw.shape[0]
    slots, steps = x_ref.shape[:2]
    across = me + 1 - 2 * lax.rem(me, 2)
    other_core = row + 1 - 2 * lax.rem(row, 2)
    other_y = lax.rem(row + 2, REQ)
    is_owner = (me >= 1) & (me <= OWNERS)
    mine = jnp.minimum(jnp.maximum(me - 1, 0), OWNERS - 1)

    loads = [
        pltpu.make_async_copy(src, dst, load_sem.at[n])
        for n, (src, dst) in enumerate(
            [(pw_hbm, pw), (ck_hbm, ck), (cv_hbm, cv), (ow_hbm, ow), (gw_hbm, gw), (uw_hbm, uw)]
        )
    ]
    dw[ff:, :] = jnp.zeros((dw.shape[0] - ff, width), dw.dtype)
    hid_ref[...] = jnp.zeros_like(hid_ref)
    loads.append(pltpu.make_async_copy(dw_hbm, dw.at[pl.ds(0, ff)], load_sem.at[6]))
    for load in loads:
        load.start()

    barrier = pltpu.get_barrier_semaphore()
    for d in range(1, SEQ):
        pl.semaphore_signal(
            barrier, inc=1, device_id={"seq": lax.rem(me + d, SEQ)}, device_id_type=MESH
        )
    pl.semaphore_signal(barrier, inc=1, device_id={"req": other_core}, device_id_type=MESH)
    pl.semaphore_signal(barrier, inc=1, device_id={"req": other_y}, device_id_type=MESH)

    def remote(src, dst, send, recv, target):
        return pltpu.make_async_remote_copy(
            src_ref=src, dst_ref=dst, send_sem=send, recv_sem=recv,
            device_id=target, device_id_type=MESH,
        )

    def rms(values, gain):
        mean_square = jnp.mean(values * values, axis=-1, keepdims=True)
        return values * lax.rsqrt(mean_square + epsilon) * gain[None, :]

    for n in range(slots):
        xs_ref[n * steps : (n + 1) * steps, :] = x_ref[n].astype(jnp.float32)
    normed = rms(xs_ref[...], g1_ref[...]).astype(jnp.bfloat16)
    cosine, sine = cos_ref[...], sin_ref[...]
    half = HD // 2
    loads[0].wait()

    def a_copy(part, k):
        target = lax.rem(me + 2 * k, SEQ) if k else across
        return remote(
            gbuf.at[me, part], gbuf.at[me, part], a_send.at[part, k], a_recv.at[me, part],
            {"seq": target},
        )

    def a_forward(part, k):
        source = lax.rem(me + 2 * k, SEQ)
        return remote(
            gbuf.at[source, part], gbuf.at[source, part], a_fwd.at[part, k - 1],
            a_recv.at[source, part], {"seq": across},
        )

    def a_arrived(source, part):
        remote(
            gbuf.at[source, part], gbuf.at[source, part], a_fwd.at[0, 0],
            a_recv.at[source, part], {"seq": across},
        ).wait_recv()

    for part in range(2):
        projected = jnp.dot(
            normed, pw[:, part * 2 * HD : (part + 1) * 2 * HD], preferred_element_type=jnp.float32
        )
        projected = projected.astype(jnp.bfloat16).astype(jnp.float32)
        for h in range(2):
            a = projected[:, h * HD : h * HD + half]
            b = projected[:, h * HD + half : (h + 1) * HD]
            gbuf[me, part, :, h * HD : h * HD + half] = (a * cosine - b * sine).astype(
                jnp.bfloat16
            )
            gbuf[me, part, :, h * HD + half : (h + 1) * HD] = (b * cosine + a * sine).astype(
                jnp.bfloat16
            )
        if part == 0:
            pl.semaphore_wait(barrier, SEQ + 1)
        for k in (2, 3, 1, 0):
            a_copy(part, k).start()
    for part in range(2):
        for k in range(1, 4):
            a_arrived(lax.rem(me + 2 * k, SEQ), part)
            a_forward(part, k).start()

    loads[1].wait()
    loads[2].wait()
    tokens = ck.shape[0]

    def pair_row(shape, axis):
        index = lax.broadcasted_iota(jnp.int32, shape, axis)
        return jnp.where(index >= rows, index - rows, index)

    owned = owner_ref[...] == pair_row((2 * rows, tokens), 0) // steps
    query_row = pair_row((2 * rows, rows), 0)
    fresh_row = lax.broadcasted_iota(jnp.int32, (2 * rows, rows), 1)
    fresh_allowed = (query_row // steps == fresh_row // steps) & (fresh_row <= query_row)
    lanes = lax.broadcasted_iota(jnp.int32, (2 * rows, 128), 1)
    totals = jnp.zeros((2 * rows, 128), jnp.float32)

    def attend(queries, keys, values, allowed):
        scores = lax.dot_general(
            queries, keys, (((1,), (1,)), ((), ())), preferred_element_type=jnp.float32
        )
        weights = jnp.where(allowed, capped_weight(scores), 0.0)
        outputs = jnp.dot(
            weights.astype(jnp.bfloat16), values, preferred_element_type=jnp.float32
        )
        return jnp.sum(weights, axis=-1, keepdims=True), outputs

    def b_copy(j):
        return remote(
            bsend.at[j - 1], brecv.at[j - 1], b_send.at[j - 1], b_recv.at[j - 1],
            {"seq": lax.rem(me + j, SEQ)},
        )

    def t_copy(j):
        return remote(
            tsend, trecv.at[j - 1], t_send.at[j - 1], t_recv.at[j - 1],
            {"seq": lax.rem(me + j, SEQ)},
        )

    for j in range(1, SEQ + 1):
        e = lax.rem(me + j, SEQ)
        block = e // 2
        part = lax.rem(e, 2)

        @pl.when(lax.rem(block, 2) != lax.rem(me, 2))
        def _():
            a_arrived(block, part)

        queries = jnp.concatenate([gbuf[block, part, :, :HD], gbuf[block, part, :, HD:]], axis=0)
        head = pl.ds(pl.multiple_of(e * HD, HD), HD)
        total, outputs = attend(queries, ck[:, head], cv[:, head], owned)
        if j < SEQ:
            bsend[j - 1] = outputs.astype(jnp.bfloat16)
            b_copy(j).start()
        else:
            for n in range(SEQ // 2, SEQ):
                @pl.when(n % 2 != lax.rem(me, 2))
                def _():
                    a_arrived(n, 0)
                    a_arrived(n, 1)

            home, lane = lax.rem(e // 2, 2), pl.ds(pl.multiple_of(lax.rem(e, 2) * HD, HD), HD)
            fresh_total, fresh_outputs = attend(
                queries, gbuf[4 + e // 4, home, :, lane], gbuf[6 + e // 4, home, :, lane],
                fresh_allowed,
            )
            total = total + fresh_total
            outputs = outputs + fresh_outputs
        totals = totals + jnp.where(lanes == e, total, 0.0)
    tot_ref[2 * rows :, :] = jnp.zeros((128 - 2 * rows, 128), jnp.float32)
    tot_ref[: 2 * rows, :] = totals
    tsend[...] = tot_ref[...].T[:KVH]
    for j in range(1, SEQ):
        t_copy(j).start()
    everyone = tsend[...]
    for j in range(1, SEQ):
        b_copy(j).wait_recv()
        t_copy(j).wait_recv()
        outputs = outputs + brecv[j - 1].astype(jnp.float32)
        everyone = everyone + trecv[j - 1]
    tot_ref[...] = jnp.zeros((128, 128), jnp.float32)
    tot_ref[:KVH, :] = everyone
    spread = tot_ref[...].T
    column = jnp.sum(jnp.where(lanes == me, spread[: 2 * rows], 0.0), axis=-1, keepdims=True)
    attended = outputs / column
    attended = jnp.concatenate([attended[:rows], attended[rows:]], axis=1).astype(jnp.bfloat16)

    loads[3].wait()
    mix = width // MIX_CHUNKS

    def c_send_to(c, d):
        target = lax.rem(me + d, SEQ)
        owner = jnp.minimum(jnp.maximum(target - 1, 0), OWNERS - 1)
        copy = remote(
            csend.at[c, owner], crecv.at[c, d - 1], c_send.at[c, d - 1], c_recv.at[c, d - 1],
            {"seq": target},
        )
        return (target >= 1) & (target <= OWNERS), copy

    for c in range(MIX_CHUNKS):
        part = jnp.dot(
            attended, ow[:, c * mix : (c + 1) * mix], preferred_element_type=jnp.float32
        )
        csend[c] = part.reshape(OWNERS, TILE, mix).astype(jnp.bfloat16)
        for d in range(1, SEQ):
            pred, copy = c_send_to(c, d)
            pl.when(pred)(copy.start)

    def d_copy(k):
        target = lax.rem(me + 2 * k, SEQ) if k else across
        return remote(
            feed.at[0, mine], feed.at[0, mine], d_send.at[k], d_recv.at[mine], {"seq": target}
        )

    def owner_of(seq):
        valid = (seq >= 1) & (seq <= OWNERS)
        return valid, jnp.minimum(jnp.maximum(seq - 1, 0), OWNERS - 1)

    def d_forward(k):
        valid, o = owner_of(lax.rem(me + 2 * k, SEQ))
        return valid, o, remote(
            feed.at[0, o], feed.at[0, o], d_fwd.at[k - 1], d_recv.at[o], {"seq": across}
        )

    @pl.when(is_owner)
    def _():
        pieces = []
        for c in range(MIX_CHUNKS):
            piece = csend[c, mine].astype(jnp.float32)
            for d in range(1, SEQ):
                c_send_to(c, d)[1].wait_recv()
                piece = piece + crecv[c, d - 1].astype(jnp.float32)
            pieces.append(piece)
        mixed = jnp.concatenate(pieces, axis=1)
        middle = xs_ref[pl.ds(pl.multiple_of(mine * TILE, TILE), TILE), :] + rms(mixed, g2_ref[...])
        mid_ref[...] = middle
        feed[0, mine] = rms(middle, g3_ref[...]).astype(jnp.bfloat16)
        for k in (2, 3, 1, 0):
            d_copy(k).start()

    def to_y(o):
        return remote(
            feed.at[0, o], feed.at[2, o], d2_send.at[0, o], d2_recv.at[0, o], {"req": other_y}
        )

    def to_core(o):
        return remote(
            feed.at[0, o], feed.at[1, o], d2_send.at[1, o], d2_recv.at[1, o], {"req": other_core}
        )

    def to_corner(o):
        return remote(
            feed.at[2, o], feed.at[3, o], d2_send.at[2, o], d2_recv.at[2, o], {"req": other_core}
        )

    def fill(q):
        lhs_ref[q * rows : (q + 1) * rows, :] = (
            feed[q].astype(jnp.float32).reshape(rows, width).astype(jnp.bfloat16)
        )

    def feed_half(n):
        block = lhs_ref[n * 2 * rows : (n + 1) * 2 * rows, :]
        nt = (((1,), (1,)), ((), ()))
        gate_part = lax.dot_general(block, gw[...], nt, preferred_element_type=jnp.float32)
        up_part = lax.dot_general(block, uw[...], nt, preferred_element_type=jnp.float32)
        hidden = (jax.nn.gelu(gate_part, approximate=True) * up_part).astype(jnp.bfloat16)
        hid_ref[n * 2 * rows : (n + 1) * 2 * rows, :ff] = hidden

    @pl.when(is_owner)
    def _():
        to_y(mine).start()
        to_core(mine).start()

    for k in range(1, 4):
        valid, o, copy = d_forward(k)

        @pl.when(valid)
        def _():
            copy.wait_recv()
            copy.start()
            to_y(o).start()
            to_core(o).start()

    for k in range(4):
        valid, o = owner_of(lax.rem(across + 2 * k, SEQ))

        @pl.when(valid)
        def _():
            remote(
                feed.at[0, o], feed.at[0, o], d_fwd.at[0], d_recv.at[o], {"seq": across}
            ).wait_recv()
            to_y(o).start()
            to_core(o).start()

    fill(0)
    for o in range(OWNERS):
        to_core(o).wait_recv()
    fill(1)
    loads[4].wait()
    loads[5].wait()
    feed_half(0)
    for o in range(OWNERS):
        to_y(o).wait_recv()
        to_corner(o).start()
    fill(2)
    for o in range(OWNERS):
        to_corner(o).wait_recv()
    fill(3)
    feed_half(1)
    loads[6].wait()
    piece_width = width // SUM_CHUNKS

    def e1_copy(c):
        return remote(
            e1send.at[c], e1recv.at[c], e1_ssem.at[c], e1_rsem.at[c], {"req": other_core}
        )

    def e2_copy(c):
        return remote(e2send.at[c], e2recv.at[c], e2_ssem.at[c], e2_rsem.at[c], {"req": other_y})

    def e3_copy(c, d):
        target = lax.rem(me + d, SEQ)
        owner = jnp.minimum(jnp.maximum(target - 1, 0), OWNERS - 1)
        copy = remote(
            e3send.at[c, owner], e3recv.at[c, d - 1], e3_ssem.at[c, d - 1], e3_rsem.at[c, d - 1],
            {"seq": target},
        )
        return (target >= 1) & (target <= OWNERS), copy

    for c in range(SUM_CHUNKS):
        part = jnp.dot(
            hid_ref[...],
            dw[:, c * piece_width : (c + 1) * piece_width],
            preferred_element_type=jnp.float32,
        )
        e1send[c, :rows] = part[rows : 2 * rows].astype(jnp.bfloat16)
        e1send[c, rows:] = part[3 * rows :].astype(jnp.bfloat16)
        part_ref[c, :rows] = part[:rows]
        part_ref[c, rows:] = part[2 * rows : 3 * rows]
        e1_copy(c).start()
    for c in range(SUM_CHUNKS):
        e1_copy(c).wait_recv()
        e2send[c] = (part_ref[c, rows:] + e1recv[c, rows:].astype(jnp.float32)).astype(
            jnp.bfloat16
        )
        e2_copy(c).start()
    for c in range(SUM_CHUNKS):
        e2_copy(c).wait_recv()
        kept = part_ref[c, :rows] + e1recv[c, :rows].astype(jnp.float32)
        kept = kept + e2recv[c].astype(jnp.float32)
        e3send[c] = kept.reshape(OWNERS, TILE, piece_width).astype(jnp.bfloat16)
        for d in range(1, SEQ):
            pred, copy = e3_copy(c, d)
            pl.when(pred)(copy.start)

    def f_copy(k):
        target = lax.rem(me + 2 * k, SEQ) if k else across
        return remote(
            res_ref.at[mine], res_ref.at[mine], f_send.at[k], f_recv.at[mine], {"seq": target}
        )

    def f_forward(k):
        valid, o = owner_of(lax.rem(me + 2 * k, SEQ))
        return valid, remote(
            res_ref.at[o], res_ref.at[o], f_fwd.at[k - 1], f_recv.at[o], {"seq": across}
        )

    @pl.when(is_owner)
    def _():
        pieces = []
        for c in range(SUM_CHUNKS):
            piece = e3send[c, mine].astype(jnp.float32)
            for d in range(1, SEQ):
                e3_copy(c, d)[1].wait_recv()
                piece = piece + e3recv[c, d - 1].astype(jnp.float32)
            pieces.append(piece)
        summed = jnp.concatenate(pieces, axis=1)
        res_ref[mine] = (mid_ref[...] + rms(summed, g4_ref[...])).astype(jnp.bfloat16)
        for k in (2, 3, 1, 0):
            f_copy(k).start()

    for k in range(1, 4):
        valid, copy = f_forward(k)

        @pl.when(valid)
        def _():
            copy.wait_recv()
            copy.start()

    for k in range(4):
        valid, o = owner_of(lax.rem(across + 2 * k, SEQ))

        @pl.when(valid)
        def _():
            remote(
                res_ref.at[o], res_ref.at[o], f_fwd.at[0], f_recv.at[o], {"seq": across}
            ).wait_recv()

    finished = res_ref[...].astype(jnp.float32).reshape(rows, width)
    for n in range(slots):
        out_ref[n] = finished[n * steps : (n + 1) * steps].astype(jnp.bfloat16)

    for d in range(1, SEQ):
        b_copy(d).wait_send()
        t_copy(d).wait_send()
        for c in range(MIX_CHUNKS):
            pred, copy = c_send_to(c, d)
            pl.when(pred)(copy.wait_send)
        for c in range(SUM_CHUNKS):
            pred, copy = e3_copy(c, d)
            pl.when(pred)(copy.wait_send)
    for part in range(2):
        for k in range(4):
            a_copy(part, k).wait_send()
        for k in range(1, 4):
            a_forward(part, k).wait_send()
    for k in range(1, 4):
        valid, _o, copy = d_forward(k)
        pl.when(valid)(copy.wait_send)
        valid, copy = f_forward(k)
        pl.when(valid)(copy.wait_send)
    for o in range(OWNERS):
        to_y(o).wait_send()
        to_core(o).wait_send()
        to_corner(o).wait_send()
    for c in range(SUM_CHUNKS):
        e1_copy(c).wait_send()
        e2_copy(c).wait_send()

    @pl.when(is_owner)
    def _():
        for k in range(4):
            d_copy(k).wait_send()
            f_copy(k).wait_send()


def fused_body(
    embedded,
    cache_keys,
    cache_values,
    token_owner,
    dealing,
    lengths,
    project_weight,
    output_weight,
    gate_weight,
    up_weight,
    down_weight,
    gain_first,
    gain_second,
    gain_third,
    gain_fourth,
):
    row_count = embedded.shape[1]
    rows = STEPS * row_count
    width = embedded.shape[2]
    tokens = cache_keys.shape[1]
    kvw = cache_keys.shape[2]
    columns = project_weight.shape[1]
    depth = output_weight.shape[0]
    ff = gate_weight.shape[1]
    ff_pad = -(-ff // 128) * 128
    mix = width // MIX_CHUNKS
    piece = width // SUM_CHUNKS
    group_index = lax.axis_index("req")
    seq_index = lax.axis_index("seq")
    slot_requests = lax.dynamic_slice_in_dim(dealing, group_index * row_count, row_count)
    matches = slot_requests[:, None] == jnp.arange(dealing.shape[0], dtype=jnp.int32)[None, :]
    base_positions = jnp.sum(jnp.where(matches, lengths[None, :], 0), axis=1)
    positions = base_positions[:, None] + jnp.arange(STEPS, dtype=jnp.int32)[None, :]
    positions = positions.reshape(rows).astype(jnp.float32)
    freq_index = jnp.arange(HD // 2, dtype=jnp.float32)
    inverse = jnp.exp(freq_index * (-2.0 * math.log(10000.0) / HD))
    angles = positions[:, None] * inverse[None, :]
    scale = jnp.where(seq_index < SEQ // 2, HD ** (-0.5), 1.0)
    turned = seq_index < 3 * SEQ // 4
    cosine = jnp.where(turned, jnp.cos(angles) * scale, 1.0)
    sine = jnp.where(turned, jnp.sin(angles) * scale, 0.0)
    bf16, f32 = jnp.bfloat16, jnp.float32
    dma = pltpu.SemaphoreType.DMA
    vmem = pl.BlockSpec(memory_space=pltpu.VMEM)
    hbm = pl.BlockSpec(memory_space=pl.ANY)
    out = pl.pallas_call(
        kernel,
        out_shape=jax.ShapeDtypeStruct((row_count, STEPS, width), bf16),
        in_specs=[vmem] * 8 + [hbm] * 7,
        out_specs=vmem,
        scratch_shapes=[
            pltpu.VMEM((width, columns), bf16),
            pltpu.VMEM((tokens, kvw), bf16),
            pltpu.VMEM((tokens, kvw), bf16),
            pltpu.VMEM((depth, width), bf16),
            pltpu.VMEM((ff, width), bf16),
            pltpu.VMEM((ff, width), bf16),
            pltpu.VMEM((ff_pad, width), bf16),
            pltpu.VMEM((rows, width), f32),
            pltpu.VMEM((OWNERS, TILE, width), bf16),
            pltpu.VMEM((SEQ, 2, rows, columns // 2), bf16),
            pltpu.VMEM((SEQ - 1, 2 * rows, HD), bf16),
            pltpu.VMEM((SEQ - 1, 2 * rows, HD), bf16),
            pltpu.VMEM((128, 128), f32),
            pltpu.VMEM((KVH, 128), f32),
            pltpu.VMEM((SEQ - 1, KVH, 128), f32),
            pltpu.VMEM((MIX_CHUNKS, OWNERS, TILE, mix), bf16),
            pltpu.VMEM((MIX_CHUNKS, SEQ - 1, TILE, mix), bf16),
            pltpu.VMEM((TILE, width), f32),
            pltpu.VMEM((REQ, OWNERS, TILE, width), bf16),
            pltpu.VMEM((REQ * rows, width), bf16),
            pltpu.VMEM((REQ * rows, ff_pad), bf16),
            pltpu.VMEM((SUM_CHUNKS, 2 * rows, piece), f32),
            pltpu.VMEM((SUM_CHUNKS, 2 * rows, piece), bf16),
            pltpu.VMEM((SUM_CHUNKS, 2 * rows, piece), bf16),
            pltpu.VMEM((SUM_CHUNKS, rows, piece), bf16),
            pltpu.VMEM((SUM_CHUNKS, rows, piece), bf16),
            pltpu.VMEM((SUM_CHUNKS, OWNERS, TILE, piece), bf16),
            pltpu.VMEM((SUM_CHUNKS, SEQ - 1, TILE, piece), bf16),
            dma((7,)),
            dma((2, 4)),
            dma((SEQ, 2)),
            dma((2, 3)),
            dma((SEQ - 1,)),
            dma((SEQ - 1,)),
            dma((SEQ - 1,)),
            dma((SEQ - 1,)),
            dma((MIX_CHUNKS, SEQ - 1)),
            dma((MIX_CHUNKS, SEQ - 1)),
            dma((4,)),
            dma((OWNERS,)),
            dma((3,)),
            dma((3, OWNERS)),
            dma((3, OWNERS)),
            dma((SUM_CHUNKS,)),
            dma((SUM_CHUNKS,)),
            dma((SUM_CHUNKS,)),
            dma((SUM_CHUNKS,)),
            dma((SUM_CHUNKS, SEQ - 1)),
            dma((SUM_CHUNKS, SEQ - 1)),
            dma((4,)),
            dma((OWNERS,)),
            dma((3,)),
        ],
        compiler_params=pltpu.CompilerParams(
            collective_id=0, has_side_effects=True, vmem_limit_bytes=58 << 20
        ),
    )(
        embedded.transpose(1, 0, 2),
        cosine,
        sine,
        token_owner,
        gain_first,
        gain_second,
        gain_third,
        gain_fourth,
        project_weight,
        cache_keys[0],
        cache_values[0],
        output_weight,
        gate_weight.T,
        up_weight.T,
        down_weight,
    )
    return out.transpose(1, 0, 2)


def body(*args):
    embedded, cache_keys = args[0], args[1]
    rows = STEPS * embedded.shape[1]
    fits = (
        lax.axis_size("seq") == SEQ
        and lax.axis_size("req") == REQ
        and rows == OWNERS * TILE
        and KVH == SEQ
        and cache_keys.shape[2] == KVH * HD
    )
    return fused_body(*args) if fits else plain_body(*args)


def solution(mesh):
    return jax.shard_map(
        body,
        mesh=mesh,
        in_specs=(
            P(None, "req", None),
            P("req", "seq", None),
            P("req", "seq", None),
            P("req", "seq"),
            P(),
            P(),
            P(None, "seq"),
            P("seq", None),
            P(None, ("req", "seq")),
            P(None, ("req", "seq")),
            P(("req", "seq"), None),
            P(),
            P(),
            P(),
            P(),
        ),
        out_specs=P(None, "req", None),
        check_vma=False,
    )
```

```python
import math

import jax
import jax.numpy as jnp
from jax import lax
from jax.experimental import pallas as pl
from jax.experimental.pallas import tpu as pltpu
from jax.sharding import PartitionSpec as P

H = 16
KVH = 8
HD = 256
STEPS = 4


soft_cap = 50.0
epsilon = 1e-06


def rms_scale(values, gain):
    mean_square = jnp.mean(values * values, axis=-1, keepdims=True)
    return values * lax.rsqrt(mean_square + epsilon) * gain


def rotate(values, positions):
    half_width = values.shape[-1] // 2
    freq_index = jnp.arange(half_width, dtype=jnp.float32)
    inverse = jnp.exp(freq_index * (-2.0 * math.log(10000.0) / values.shape[-1]))
    angles = positions[:, None] * inverse[None, :]
    cosine = jnp.cos(angles)[:, None, :]
    sine = jnp.sin(angles)[:, None, :]
    first_half = values[..., :half_width]
    second_half = values[..., half_width:]
    return jnp.concatenate(
        [first_half * cosine - second_half * sine, second_half * cosine + first_half * sine],
        axis=-1,
    )


def capped_weight(scores):
    return jnp.exp(soft_cap * jnp.tanh(scores / soft_cap))


def rounded(values):
    return lax.optimization_barrier(values.astype(jnp.bfloat16)).astype(jnp.float32)


def plain_body(
    embedded,
    cache_keys,
    cache_values,
    token_owner,
    dealing,
    lengths,
    project_weight,
    output_weight,
    gate_weight,
    up_weight,
    down_weight,
    gain_first,
    gain_second,
    gain_third,
    gain_fourth,
):
    row_count = embedded.shape[1]
    rows = STEPS * row_count
    width = embedded.shape[2]
    local_tokens = cache_keys.shape[1]
    value_width = cache_keys.shape[2]
    group_size = H // KVH
    attention_width = H * HD
    column_count = output_weight.shape[0]
    group_index = lax.axis_index("req")
    seq_index = lax.axis_index("seq")
    seq_size = lax.axis_size("seq")
    req_size = lax.axis_size("req")
    column_start = seq_index * column_count
    slot_requests = lax.dynamic_slice_in_dim(dealing, group_index * row_count, row_count)
    matches = slot_requests[:, None] == jnp.arange(dealing.shape[0], dtype=jnp.int32)[None, :]
    base_positions = jnp.sum(jnp.where(matches, lengths[None, :], 0), axis=1)
    positions = base_positions[None, :] + jnp.arange(STEPS, dtype=jnp.int32)[:, None]
    positions = positions.reshape(rows).astype(jnp.float32)
    key_pool = cache_keys[0].reshape(local_tokens, KVH, HD)
    value_pool = cache_values[0].reshape(local_tokens, KVH, HD)
    slots = jnp.tile(jnp.arange(row_count, dtype=jnp.int32), STEPS)
    moments = jnp.repeat(jnp.arange(STEPS, dtype=jnp.int32), row_count)
    owned_mask = token_owner[0][None, :] == slots[:, None]
    stream = embedded.reshape(rows, width).astype(jnp.float32)
    normed = rms_scale(stream, gain_first).astype(jnp.bfloat16)
    local_part = jnp.dot(normed, project_weight, preferred_element_type=jnp.float32).astype(
        jnp.bfloat16
    )
    projected = lax.all_gather(local_part, "seq", axis=1, tiled=True)
    query_rows = projected[:, :attention_width].astype(jnp.float32).reshape(rows, H, HD)
    queries = (rotate(query_rows, positions) * HD ** (-0.5)).astype(jnp.bfloat16)
    key_rows = (
        projected[:, attention_width : attention_width + value_width]
        .astype(jnp.float32)
        .reshape(rows, KVH, HD)
    )
    fresh_keys = rotate(key_rows, positions).astype(jnp.bfloat16)
    fresh_values = projected[:, attention_width + value_width :].reshape(rows, KVH, HD)
    grouped = queries.reshape(rows, KVH, group_size, HD)
    all_keys = jnp.concatenate([key_pool, fresh_keys], axis=0)
    all_values = jnp.concatenate([value_pool, fresh_values], axis=0)
    fresh_mask = (
        (slots[None, :] == slots[:, None])
        & (moments[None, :] <= moments[:, None])
        & (seq_index == 0)
    )
    mask = jnp.concatenate([owned_mask, fresh_mask], axis=1)
    scores = jnp.einsum("igqd,tgd->igqt", grouped, all_keys, preferred_element_type=jnp.float32)
    weights = jnp.where(mask[:, None, None, :], capped_weight(scores), 0.0)
    totals = lax.psum(jnp.sum(weights, axis=-1), "seq").reshape(rows, H)
    outputs = jnp.einsum(
        "igqt,tgd->igqd",
        weights.astype(jnp.bfloat16),
        all_values,
        preferred_element_type=jnp.float32,
    ).reshape(rows, attention_width)
    outputs = lax.psum_scatter(outputs, "seq", scatter_dimension=1, tiled=True)
    spread = jnp.repeat(totals, HD, axis=1)
    spread = lax.dynamic_slice_in_dim(spread, column_start, column_count, 1)
    attended = (outputs / spread).astype(jnp.bfloat16)
    partial = jnp.dot(attended, output_weight, preferred_element_type=jnp.float32)
    mixed = lax.psum(partial, "seq")
    middle = stream + rms_scale(mixed, gain_second)
    feed_input = rms_scale(middle, gain_third).astype(jnp.bfloat16)
    block_rows = lax.all_gather(feed_input, "req", axis=0, tiled=True)
    gate_part = jnp.dot(block_rows, gate_weight, preferred_element_type=jnp.float32)
    up_part = jnp.dot(block_rows, up_weight, preferred_element_type=jnp.float32)
    hidden = (jax.nn.gelu(gate_part, approximate=True) * up_part).astype(jnp.bfloat16)
    summed = jnp.dot(hidden, down_weight, preferred_element_type=jnp.float32)
    summed = lax.psum_scatter(summed, "req", scatter_dimension=0, tiled=True)
    summed = lax.psum(summed, "seq")
    results = (middle + rms_scale(summed, gain_fourth)).astype(jnp.bfloat16)
    return results.reshape(STEPS, row_count, width)


MESH = pl.DeviceIdType.MESH
SEQ = 8
REQ = 4
OWNERS = 6
TILE = 8
MIX_CHUNKS = 2
SUM_CHUNKS = 4


def kernel(
    x_ref, cos_ref, sin_ref, owner_ref, g1_ref, g2_ref, g3_ref, g4_ref,
    pw_hbm, ck_hbm, cv_hbm, ow_hbm, gw_hbm, uw_hbm, dw_hbm,
    out_ref,
    pw, ck, cv, ow, gw, uw, dw,
    xs_ref, res_ref, gbuf, bsend, brecv, bzsend, bzrecv, tot_ref, tsend, trecv, csend, crecv, mid_ref, feed, lhs_ref, hid_ref,
    part_ref, e1send, e1recv, e2send, e2recv, e3send, e3recv,
    load_sem, a_send, a_recv, a_fwd, b_send, b_recv, bz_send, bz_recv, t_send, t_recv, c_send, c_recv,
    d_send, d_recv, d_fwd, d2_send, d2_recv, e1_ssem, e1_rsem, e2_ssem, e2_rsem, e3_ssem, e3_rsem,
    f_send, f_recv, f_fwd,
):
    me = lax.axis_index("seq")
    row = lax.axis_index("req")
    width = x_ref.shape[2]
    rows = OWNERS * TILE
    ff = gw.shape[0]
    slots, steps = x_ref.shape[:2]
    across = me + 1 - 2 * lax.rem(me, 2)
    other_core = row + 1 - 2 * lax.rem(row, 2)
    other_y = lax.rem(row + 2, REQ)
    is_owner = (me >= 1) & (me <= OWNERS)
    mine = jnp.minimum(jnp.maximum(me - 1, 0), OWNERS - 1)

    loads = [
        pltpu.make_async_copy(src, dst, load_sem.at[n])
        for n, (src, dst) in enumerate(
            [(pw_hbm.at[:, pl.ds(0, 2 * HD)], pw.at[0]), (ck_hbm, ck), (cv_hbm, cv), (ow_hbm, ow),
             (gw_hbm, gw), (uw_hbm, uw)]
        )
    ]
    loads.append(pltpu.make_async_copy(dw_hbm, dw.at[pl.ds(0, ff)], load_sem.at[6]))
    loads.append(
        pltpu.make_async_copy(pw_hbm.at[:, pl.ds(2 * HD, 2 * HD)], pw.at[1], load_sem.at[7])
    )
    loads[0].start()
    loads[7].start()

    barrier = pltpu.get_barrier_semaphore()
    for d in range(1, SEQ):
        pl.semaphore_signal(
            barrier, inc=1, device_id={"seq": lax.rem(me + d, SEQ)}, device_id_type=MESH
        )
    pl.semaphore_signal(barrier, inc=1, device_id={"req": other_core}, device_id_type=MESH)
    pl.semaphore_signal(barrier, inc=1, device_id={"req": other_y}, device_id_type=MESH)

    def remote(src, dst, send, recv, target):
        return pltpu.make_async_remote_copy(
            src_ref=src, dst_ref=dst, send_sem=send, recv_sem=recv,
            device_id=target, device_id_type=MESH,
        )

    def rms(values, gain):
        mean_square = jnp.mean(values * values, axis=-1, keepdims=True)
        return values * lax.rsqrt(mean_square + epsilon) * gain[None, :]

    for n in range(slots):
        xs_ref[n * steps : (n + 1) * steps, :] = x_ref[n].astype(jnp.float32)
    normed = rms(xs_ref[...], g1_ref[...]).astype(jnp.bfloat16)
    cosine, sine = cos_ref[...], sin_ref[...]
    half = HD // 2
    dw[ff:, :] = jnp.zeros((dw.shape[0] - ff, width), dw.dtype)
    hid_ref[...] = jnp.zeros_like(hid_ref)

    def a_copy(part, k):
        target = lax.rem(me + 2 * k, SEQ) if k else across
        return remote(
            gbuf.at[me, part], gbuf.at[me, part], a_send.at[part, k], a_recv.at[me, part],
            {"seq": target},
        )

    def a_forward(part, k):
        source = lax.rem(me + 2 * k, SEQ)
        return remote(
            gbuf.at[source, part], gbuf.at[source, part], a_fwd.at[part, k - 1],
            a_recv.at[source, part], {"seq": across},
        )

    def a_arrived(source, part):
        remote(
            gbuf.at[source, part], gbuf.at[source, part], a_fwd.at[0, 0],
            a_recv.at[source, part], {"seq": across},
        ).wait_recv()

    for part in range(2):
        loads[7 if part else 0].wait()
        if part:
            for n in range(1, 7):
                loads[n].start()
        projected = jnp.dot(normed, pw[part], preferred_element_type=jnp.float32)
        projected = projected.astype(jnp.bfloat16).astype(jnp.float32)
        for h in range(2):
            a = projected[:, h * HD : h * HD + half]
            b = projected[:, h * HD + half : (h + 1) * HD]
            gbuf[me, part, :, h * HD : h * HD + half] = (a * cosine - b * sine).astype(
                jnp.bfloat16
            )
            gbuf[me, part, :, h * HD + half : (h + 1) * HD] = (b * cosine + a * sine).astype(
                jnp.bfloat16
            )
        if part == 0:
            pl.semaphore_wait(barrier, SEQ + 1)
        for k in (2, 3, 1, 0):
            a_copy(part, k).start()
    for part in range(2):
        for k in range(1, 4):
            a_arrived(lax.rem(me + 2 * k, SEQ), part)
            a_forward(part, k).start()

    loads[1].wait()
    loads[2].wait()
    tokens = ck.shape[0]

    def pair_row(shape, axis):
        index = lax.broadcasted_iota(jnp.int32, shape, axis)
        return jnp.where(index >= rows, index - rows, index)

    owned = owner_ref[...] == pair_row((2 * rows, tokens), 0) // steps
    query_row = pair_row((2 * rows, rows), 0)
    fresh_row = lax.broadcasted_iota(jnp.int32, (2 * rows, rows), 1)
    fresh_allowed = (query_row // steps == fresh_row // steps) & (fresh_row <= query_row)
    lanes = lax.broadcasted_iota(jnp.int32, (2 * rows, 128), 1)
    totals = jnp.zeros((2 * rows, 128), jnp.float32)

    def attend(queries, keys, values, allowed):
        scores = lax.dot_general(
            queries, keys, (((1,), (1,)), ((), ())), preferred_element_type=jnp.float32
        )
        weights = jnp.where(allowed, capped_weight(scores), 0.0)
        outputs = jnp.dot(
            weights.astype(jnp.bfloat16), values, preferred_element_type=jnp.float32
        )
        return jnp.sum(weights, axis=-1, keepdims=True), outputs

    def b_copy(k):
        return remote(bsend.at[k], brecv.at[k], b_send.at[k], b_recv.at[k], {"seq": across})

    def bz_copy(k):
        return remote(
            bzsend.at[k - 1], bzrecv.at[k - 1], bz_send.at[k - 1], bz_recv.at[k - 1],
            {"seq": lax.rem(me + 2 * k, SEQ)},
        )

    def t_copy(j):
        return remote(
            tsend, trecv.at[j - 1], t_send.at[j - 1], t_recv.at[j - 1],
            {"seq": lax.rem(me + j, SEQ)},
        )

    for side, k in [(across, 2), (across, 3), (across, 1), (across, 0),
                    (me, 2), (me, 3), (me, 1), (me, 0)]:
        e = lax.rem(side + 2 * k, SEQ)
        block = e // 2
        part = lax.rem(e, 2)

        @pl.when(lax.rem(block, 2) != lax.rem(me, 2))
        def _():
            a_arrived(block, part)

        queries = jnp.concatenate([gbuf[block, part, :, :HD], gbuf[block, part, :, HD:]], axis=0)
        head = pl.ds(pl.multiple_of(e * HD, HD), HD)
        total, outputs = attend(queries, ck[:, head], cv[:, head], owned)
        if side is across:
            bsend[k] = outputs.astype(jnp.bfloat16)
            b_copy(k).start()
        elif k:
            b_copy(k).wait_recv()
            bzsend[k - 1] = (outputs + brecv[k].astype(jnp.float32)).astype(jnp.bfloat16)
            bz_copy(k).start()
        else:
            for n in range(SEQ // 2, SEQ):
                @pl.when(n % 2 != lax.rem(me, 2))
                def _():
                    a_arrived(n, 0)
                    a_arrived(n, 1)

            home, lane = lax.rem(e // 2, 2), pl.ds(pl.multiple_of(lax.rem(e, 2) * HD, HD), HD)
            fresh_total, fresh_outputs = attend(
                queries, gbuf[4 + e // 4, home, :, lane], gbuf[6 + e // 4, home, :, lane],
                fresh_allowed,
            )
            total = total + fresh_total
            outputs = outputs + fresh_outputs
        totals = totals + jnp.where(lanes == e, total, 0.0)
    tot_ref[2 * rows :, :] = jnp.zeros((128 - 2 * rows, 128), jnp.float32)
    tot_ref[: 2 * rows, :] = totals
    tsend[...] = tot_ref[...].T[:KVH]
    for j in range(1, SEQ):
        t_copy(j).start()
    everyone = tsend[...]
    b_copy(0).wait_recv()
    outputs = outputs + brecv[0].astype(jnp.float32)
    for k in range(1, 4):
        bz_copy(k).wait_recv()
        outputs = outputs + bzrecv[k - 1].astype(jnp.float32)
    for j in range(1, SEQ):
        t_copy(j).wait_recv()
        everyone = everyone + trecv[j - 1]
    tot_ref[...] = jnp.zeros((128, 128), jnp.float32)
    tot_ref[:KVH, :] = everyone
    spread = tot_ref[...].T
    column = jnp.sum(jnp.where(lanes == me, spread[: 2 * rows], 0.0), axis=-1, keepdims=True)
    attended = outputs / column
    attended = jnp.concatenate([attended[:rows], attended[rows:]], axis=1).astype(jnp.bfloat16)

    loads[3].wait()
    mix = width // MIX_CHUNKS

    def c_send_to(c, d):
        target = lax.rem(me + d, SEQ)
        owner = jnp.minimum(jnp.maximum(target - 1, 0), OWNERS - 1)
        copy = remote(
            csend.at[c, owner], crecv.at[c, d - 1], c_send.at[c, d - 1], c_recv.at[c, d - 1],
            {"seq": target},
        )
        return (target >= 1) & (target <= OWNERS), copy

    for c in range(MIX_CHUNKS):
        part = jnp.dot(
            attended, ow[:, c * mix : (c + 1) * mix], preferred_element_type=jnp.float32
        )
        csend[c] = part.reshape(OWNERS, TILE, mix).astype(jnp.bfloat16)
        for d in range(1, SEQ):
            pred, copy = c_send_to(c, d)
            pl.when(pred)(copy.start)

    def d_copy(k):
        target = lax.rem(me + 2 * k, SEQ) if k else across
        return remote(
            feed.at[0, mine], feed.at[0, mine], d_send.at[k], d_recv.at[mine], {"seq": target}
        )

    def owner_of(seq):
        valid = (seq >= 1) & (seq <= OWNERS)
        return valid, jnp.minimum(jnp.maximum(seq - 1, 0), OWNERS - 1)

    def d_forward(k):
        valid, o = owner_of(lax.rem(me + 2 * k, SEQ))
        return valid, o, remote(
            feed.at[0, o], feed.at[0, o], d_fwd.at[k - 1], d_recv.at[o], {"seq": across}
        )

    @pl.when(is_owner)
    def _():
        pieces = []
        for c in range(MIX_CHUNKS):
            piece = csend[c, mine].astype(jnp.float32)
            for d in range(1, SEQ):
                c_send_to(c, d)[1].wait_recv()
                piece = piece + crecv[c, d - 1].astype(jnp.float32)
            pieces.append(piece)
        mixed = jnp.concatenate(pieces, axis=1)
        middle = xs_ref[pl.ds(pl.multiple_of(mine * TILE, TILE), TILE), :] + rms(mixed, g2_ref[...])
        mid_ref[...] = middle
        feed[0, mine] = rms(middle, g3_ref[...]).astype(jnp.bfloat16)
        for k in (2, 3, 1, 0):
            d_copy(k).start()

    def to_y(o):
        return remote(
            feed.at[0, o], feed.at[2, o], d2_send.at[0, o], d2_recv.at[0, o], {"req": other_y}
        )

    def to_core(o):
        return remote(
            feed.at[0, o], feed.at[1, o], d2_send.at[1, o], d2_recv.at[1, o], {"req": other_core}
        )

    def to_corner(o):
        return remote(
            feed.at[2, o], feed.at[3, o], d2_send.at[2, o], d2_recv.at[2, o], {"req": other_core}
        )

    def fill(q):
        lhs_ref[q * rows : (q + 1) * rows, :] = (
            feed[q].astype(jnp.float32).reshape(rows, width).astype(jnp.bfloat16)
        )

    def feed_half(n):
        block = lhs_ref[n * 2 * rows : (n + 1) * 2 * rows, :]
        nt = (((1,), (1,)), ((), ()))
        gate_part = lax.dot_general(block, gw[...], nt, preferred_element_type=jnp.float32)
        up_part = lax.dot_general(block, uw[...], nt, preferred_element_type=jnp.float32)
        hidden = (jax.nn.gelu(gate_part, approximate=True) * up_part).astype(jnp.bfloat16)
        hid_ref[n * 2 * rows : (n + 1) * 2 * rows, :ff] = hidden

    @pl.when(is_owner)
    def _():
        to_y(mine).start()
        to_core(mine).start()

    for k in range(1, 4):
        valid, o, copy = d_forward(k)

        @pl.when(valid)
        def _():
            copy.wait_recv()
            copy.start()
            to_y(o).start()
            to_core(o).start()

    for k in range(4):
        valid, o = owner_of(lax.rem(across + 2 * k, SEQ))

        @pl.when(valid)
        def _():
            remote(
                feed.at[0, o], feed.at[0, o], d_fwd.at[0], d_recv.at[o], {"seq": across}
            ).wait_recv()
            to_y(o).start()
            to_core(o).start()

    fill(0)
    for o in range(OWNERS):
        to_core(o).wait_recv()
    fill(1)
    loads[4].wait()
    loads[5].wait()
    feed_half(0)
    for o in range(OWNERS):
        to_y(o).wait_recv()
        to_corner(o).start()
    fill(2)
    for o in range(OWNERS):
        to_corner(o).wait_recv()
    fill(3)
    feed_half(1)
    loads[6].wait()
    piece_width = width // SUM_CHUNKS

    def e1_copy(c):
        return remote(
            e1send.at[c], e1recv.at[c], e1_ssem.at[c], e1_rsem.at[c], {"req": other_core}
        )

    def e2_copy(c):
        return remote(e2send.at[c], e2recv.at[c], e2_ssem.at[c], e2_rsem.at[c], {"req": other_y})

    def e3_copy(c, d):
        target = lax.rem(me + d, SEQ)
        owner = jnp.minimum(jnp.maximum(target - 1, 0), OWNERS - 1)
        copy = remote(
            e3send.at[c, owner], e3recv.at[c, d - 1], e3_ssem.at[c, d - 1], e3_rsem.at[c, d - 1],
            {"seq": target},
        )
        return (target >= 1) & (target <= OWNERS), copy

    for c in range(SUM_CHUNKS):
        part = jnp.dot(
            hid_ref[...],
            dw[:, c * piece_width : (c + 1) * piece_width],
            preferred_element_type=jnp.float32,
        )
        e1send[c, :rows] = part[rows : 2 * rows].astype(jnp.bfloat16)
        e1send[c, rows:] = part[3 * rows :].astype(jnp.bfloat16)
        part_ref[c, :rows] = part[:rows]
        part_ref[c, rows:] = part[2 * rows : 3 * rows]
        e1_copy(c).start()
    for c in range(SUM_CHUNKS):
        e1_copy(c).wait_recv()
        e2send[c] = (part_ref[c, rows:] + e1recv[c, rows:].astype(jnp.float32)).astype(
            jnp.bfloat16
        )
        e2_copy(c).start()
    for c in range(SUM_CHUNKS):
        e2_copy(c).wait_recv()
        kept = part_ref[c, :rows] + e1recv[c, :rows].astype(jnp.float32)
        kept = kept + e2recv[c].astype(jnp.float32)
        e3send[c] = kept.reshape(OWNERS, TILE, piece_width).astype(jnp.bfloat16)
        for d in range(1, SEQ):
            pred, copy = e3_copy(c, d)
            pl.when(pred)(copy.start)

    def f_copy(k):
        target = lax.rem(me + 2 * k, SEQ) if k else across
        return remote(
            res_ref.at[mine], res_ref.at[mine], f_send.at[k], f_recv.at[mine], {"seq": target}
        )

    def f_forward(k):
        valid, o = owner_of(lax.rem(me + 2 * k, SEQ))
        return valid, remote(
            res_ref.at[o], res_ref.at[o], f_fwd.at[k - 1], f_recv.at[o], {"seq": across}
        )

    @pl.when(is_owner)
    def _():
        pieces = []
        for c in range(SUM_CHUNKS):
            piece = e3send[c, mine].astype(jnp.float32)
            for d in range(1, SEQ):
                e3_copy(c, d)[1].wait_recv()
                piece = piece + e3recv[c, d - 1].astype(jnp.float32)
            pieces.append(piece)
        summed = jnp.concatenate(pieces, axis=1)
        res_ref[mine] = (mid_ref[...] + rms(summed, g4_ref[...])).astype(jnp.bfloat16)
        for k in (2, 3, 1, 0):
            f_copy(k).start()

    for k in range(1, 4):
        valid, copy = f_forward(k)

        @pl.when(valid)
        def _():
            copy.wait_recv()
            copy.start()

    for k in range(4):
        valid, o = owner_of(lax.rem(across + 2 * k, SEQ))

        @pl.when(valid)
        def _():
            remote(
                res_ref.at[o], res_ref.at[o], f_fwd.at[0], f_recv.at[o], {"seq": across}
            ).wait_recv()

    finished = res_ref[...].astype(jnp.float32).reshape(rows, width)
    for n in range(slots):
        out_ref[n] = finished[n * steps : (n + 1) * steps].astype(jnp.bfloat16)

    for d in range(1, SEQ):
        t_copy(d).wait_send()
        for c in range(MIX_CHUNKS):
            pred, copy = c_send_to(c, d)
            pl.when(pred)(copy.wait_send)
        for c in range(SUM_CHUNKS):
            pred, copy = e3_copy(c, d)
            pl.when(pred)(copy.wait_send)
    for k in range(4):
        b_copy(k).wait_send()
    for k in range(1, 4):
        bz_copy(k).wait_send()
    for part in range(2):
        for k in range(4):
            a_copy(part, k).wait_send()
        for k in range(1, 4):
            a_forward(part, k).wait_send()
    for k in range(1, 4):
        valid, _o, copy = d_forward(k)
        pl.when(valid)(copy.wait_send)
        valid, copy = f_forward(k)
        pl.when(valid)(copy.wait_send)
    for o in range(OWNERS):
        to_y(o).wait_send()
        to_core(o).wait_send()
        to_corner(o).wait_send()
    for c in range(SUM_CHUNKS):
        e1_copy(c).wait_send()
        e2_copy(c).wait_send()

    @pl.when(is_owner)
    def _():
        for k in range(4):
            d_copy(k).wait_send()
            f_copy(k).wait_send()


def fused_body(
    embedded,
    cache_keys,
    cache_values,
    token_owner,
    dealing,
    lengths,
    project_weight,
    output_weight,
    gate_weight,
    up_weight,
    down_weight,
    gain_first,
    gain_second,
    gain_third,
    gain_fourth,
):
    row_count = embedded.shape[1]
    rows = STEPS * row_count
    width = embedded.shape[2]
    tokens = cache_keys.shape[1]
    kvw = cache_keys.shape[2]
    columns = project_weight.shape[1]
    depth = output_weight.shape[0]
    ff = gate_weight.shape[1]
    ff_pad = -(-ff // 128) * 128
    mix = width // MIX_CHUNKS
    piece = width // SUM_CHUNKS
    group_index = lax.axis_index("req")
    seq_index = lax.axis_index("seq")
    slot_requests = lax.dynamic_slice_in_dim(dealing, group_index * row_count, row_count)
    matches = slot_requests[:, None] == jnp.arange(dealing.shape[0], dtype=jnp.int32)[None, :]
    base_positions = jnp.sum(jnp.where(matches, lengths[None, :], 0), axis=1)
    positions = base_positions[:, None] + jnp.arange(STEPS, dtype=jnp.int32)[None, :]
    positions = positions.reshape(rows).astype(jnp.float32)
    freq_index = jnp.arange(HD // 2, dtype=jnp.float32)
    inverse = jnp.exp(freq_index * (-2.0 * math.log(10000.0) / HD))
    angles = positions[:, None] * inverse[None, :]
    scale = jnp.where(seq_index < SEQ // 2, HD ** (-0.5), 1.0)
    turned = seq_index < 3 * SEQ // 4
    cosine = jnp.where(turned, jnp.cos(angles) * scale, 1.0)
    sine = jnp.where(turned, jnp.sin(angles) * scale, 0.0)
    bf16, f32 = jnp.bfloat16, jnp.float32
    dma = pltpu.SemaphoreType.DMA
    vmem = pl.BlockSpec(memory_space=pltpu.VMEM)
    hbm = pl.BlockSpec(memory_space=pl.ANY)
    out = pl.pallas_call(
        kernel,
        out_shape=jax.ShapeDtypeStruct((row_count, STEPS, width), bf16),
        in_specs=[vmem] * 8 + [hbm] * 7,
        out_specs=vmem,
        scratch_shapes=[
            pltpu.VMEM((2, width, columns // 2), bf16),
            pltpu.VMEM((tokens, kvw), bf16),
            pltpu.VMEM((tokens, kvw), bf16),
            pltpu.VMEM((depth, width), bf16),
            pltpu.VMEM((ff, width), bf16),
            pltpu.VMEM((ff, width), bf16),
            pltpu.VMEM((ff_pad, width), bf16),
            pltpu.VMEM((rows, width), f32),
            pltpu.VMEM((OWNERS, TILE, width), bf16),
            pltpu.VMEM((SEQ, 2, rows, columns // 2), bf16),
            pltpu.VMEM((4, 2 * rows, HD), bf16),
            pltpu.VMEM((4, 2 * rows, HD), bf16),
            pltpu.VMEM((3, 2 * rows, HD), bf16),
            pltpu.VMEM((3, 2 * rows, HD), bf16),
            pltpu.VMEM((128, 128), f32),
            pltpu.VMEM((KVH, 128), f32),
            pltpu.VMEM((SEQ - 1, KVH, 128), f32),
            pltpu.VMEM((MIX_CHUNKS, OWNERS, TILE, mix), bf16),
            pltpu.VMEM((MIX_CHUNKS, SEQ - 1, TILE, mix), bf16),
            pltpu.VMEM((TILE, width), f32),
            pltpu.VMEM((REQ, OWNERS, TILE, width), bf16),
            pltpu.VMEM((REQ * rows, width), bf16),
            pltpu.VMEM((REQ * rows, ff_pad), bf16),
            pltpu.VMEM((SUM_CHUNKS, 2 * rows, piece), f32),
            pltpu.VMEM((SUM_CHUNKS, 2 * rows, piece), bf16),
            pltpu.VMEM((SUM_CHUNKS, 2 * rows, piece), bf16),
            pltpu.VMEM((SUM_CHUNKS, rows, piece), bf16),
            pltpu.VMEM((SUM_CHUNKS, rows, piece), bf16),
            pltpu.VMEM((SUM_CHUNKS, OWNERS, TILE, piece), bf16),
            pltpu.VMEM((SUM_CHUNKS, SEQ - 1, TILE, piece), bf16),
            dma((8,)),
            dma((2, 4)),
            dma((SEQ, 2)),
            dma((2, 3)),
            dma((4,)),
            dma((4,)),
            dma((3,)),
            dma((3,)),
            dma((SEQ - 1,)),
            dma((SEQ - 1,)),
            dma((MIX_CHUNKS, SEQ - 1)),
            dma((MIX_CHUNKS, SEQ - 1)),
            dma((4,)),
            dma((OWNERS,)),
            dma((3,)),
            dma((3, OWNERS)),
            dma((3, OWNERS)),
            dma((SUM_CHUNKS,)),
            dma((SUM_CHUNKS,)),
            dma((SUM_CHUNKS,)),
            dma((SUM_CHUNKS,)),
            dma((SUM_CHUNKS, SEQ - 1)),
            dma((SUM_CHUNKS, SEQ - 1)),
            dma((4,)),
            dma((OWNERS,)),
            dma((3,)),
        ],
        compiler_params=pltpu.CompilerParams(
            collective_id=0, has_side_effects=True, vmem_limit_bytes=58 << 20
        ),
    )(
        embedded.transpose(1, 0, 2),
        cosine,
        sine,
        token_owner,
        gain_first,
        gain_second,
        gain_third,
        gain_fourth,
        project_weight,
        cache_keys[0],
        cache_values[0],
        output_weight,
        gate_weight.T,
        up_weight.T,
        down_weight,
    )
    return out.transpose(1, 0, 2)


def body(*args):
    embedded, cache_keys = args[0], args[1]
    rows = STEPS * embedded.shape[1]
    fits = (
        lax.axis_size("seq") == SEQ
        and lax.axis_size("req") == REQ
        and rows == OWNERS * TILE
        and KVH == SEQ
        and cache_keys.shape[2] == KVH * HD
    )
    return fused_body(*args) if fits else plain_body(*args)


def solution(mesh):
    return jax.shard_map(
        body,
        mesh=mesh,
        in_specs=(
            P(None, "req", None),
            P("req", "seq", None),
            P("req", "seq", None),
            P("req", "seq"),
            P(),
            P(),
            P(None, "seq"),
            P("seq", None),
            P(None, ("req", "seq")),
            P(None, ("req", "seq")),
            P(("req", "seq"), None),
            P(),
            P(),
            P(),
            P(),
        ),
        out_specs=P(None, "req", None),
        check_vma=False,
    )
```

```python
import math

import jax
import jax.numpy as jnp
from jax import lax
from jax.experimental import pallas as pl
from jax.experimental.pallas import tpu as pltpu
from jax.sharding import PartitionSpec as P

H = 16
KVH = 8
HD = 256
STEPS = 4


soft_cap = 50.0
epsilon = 1e-06


def rms_scale(values, gain):
    mean_square = jnp.mean(values * values, axis=-1, keepdims=True)
    return values * lax.rsqrt(mean_square + epsilon) * gain


def rotate(values, positions):
    half_width = values.shape[-1] // 2
    freq_index = jnp.arange(half_width, dtype=jnp.float32)
    inverse = jnp.exp(freq_index * (-2.0 * math.log(10000.0) / values.shape[-1]))
    angles = positions[:, None] * inverse[None, :]
    cosine = jnp.cos(angles)[:, None, :]
    sine = jnp.sin(angles)[:, None, :]
    first_half = values[..., :half_width]
    second_half = values[..., half_width:]
    return jnp.concatenate(
        [first_half * cosine - second_half * sine, second_half * cosine + first_half * sine],
        axis=-1,
    )


def capped_weight(scores):
    return jnp.exp(soft_cap * jnp.tanh(scores / soft_cap))


def rounded(values):
    return lax.optimization_barrier(values.astype(jnp.bfloat16)).astype(jnp.float32)


def plain_body(
    embedded,
    cache_keys,
    cache_values,
    token_owner,
    dealing,
    lengths,
    project_weight,
    output_weight,
    gate_weight,
    up_weight,
    down_weight,
    gain_first,
    gain_second,
    gain_third,
    gain_fourth,
):
    row_count = embedded.shape[1]
    rows = STEPS * row_count
    width = embedded.shape[2]
    local_tokens = cache_keys.shape[1]
    value_width = cache_keys.shape[2]
    group_size = H // KVH
    attention_width = H * HD
    column_count = output_weight.shape[0]
    group_index = lax.axis_index("req")
    seq_index = lax.axis_index("seq")
    seq_size = lax.axis_size("seq")
    req_size = lax.axis_size("req")
    column_start = seq_index * column_count
    slot_requests = lax.dynamic_slice_in_dim(dealing, group_index * row_count, row_count)
    matches = slot_requests[:, None] == jnp.arange(dealing.shape[0], dtype=jnp.int32)[None, :]
    base_positions = jnp.sum(jnp.where(matches, lengths[None, :], 0), axis=1)
    positions = base_positions[None, :] + jnp.arange(STEPS, dtype=jnp.int32)[:, None]
    positions = positions.reshape(rows).astype(jnp.float32)
    key_pool = cache_keys[0].reshape(local_tokens, KVH, HD)
    value_pool = cache_values[0].reshape(local_tokens, KVH, HD)
    slots = jnp.tile(jnp.arange(row_count, dtype=jnp.int32), STEPS)
    moments = jnp.repeat(jnp.arange(STEPS, dtype=jnp.int32), row_count)
    owned_mask = token_owner[0][None, :] == slots[:, None]
    stream = embedded.reshape(rows, width).astype(jnp.float32)
    normed = rms_scale(stream, gain_first).astype(jnp.bfloat16)
    local_part = jnp.dot(normed, project_weight, preferred_element_type=jnp.float32).astype(
        jnp.bfloat16
    )
    projected = lax.all_gather(local_part, "seq", axis=1, tiled=True)
    query_rows = projected[:, :attention_width].astype(jnp.float32).reshape(rows, H, HD)
    queries = (rotate(query_rows, positions) * HD ** (-0.5)).astype(jnp.bfloat16)
    key_rows = (
        projected[:, attention_width : attention_width + value_width]
        .astype(jnp.float32)
        .reshape(rows, KVH, HD)
    )
    fresh_keys = rotate(key_rows, positions).astype(jnp.bfloat16)
    fresh_values = projected[:, attention_width + value_width :].reshape(rows, KVH, HD)
    grouped = queries.reshape(rows, KVH, group_size, HD)
    all_keys = jnp.concatenate([key_pool, fresh_keys], axis=0)
    all_values = jnp.concatenate([value_pool, fresh_values], axis=0)
    fresh_mask = (
        (slots[None, :] == slots[:, None])
        & (moments[None, :] <= moments[:, None])
        & (seq_index == 0)
    )
    mask = jnp.concatenate([owned_mask, fresh_mask], axis=1)
    scores = jnp.einsum("igqd,tgd->igqt", grouped, all_keys, preferred_element_type=jnp.float32)
    weights = jnp.where(mask[:, None, None, :], capped_weight(scores), 0.0)
    totals = lax.psum(jnp.sum(weights, axis=-1), "seq").reshape(rows, H)
    outputs = jnp.einsum(
        "igqt,tgd->igqd",
        weights.astype(jnp.bfloat16),
        all_values,
        preferred_element_type=jnp.float32,
    ).reshape(rows, attention_width)
    outputs = lax.psum_scatter(outputs, "seq", scatter_dimension=1, tiled=True)
    spread = jnp.repeat(totals, HD, axis=1)
    spread = lax.dynamic_slice_in_dim(spread, column_start, column_count, 1)
    attended = (outputs / spread).astype(jnp.bfloat16)
    partial = jnp.dot(attended, output_weight, preferred_element_type=jnp.float32)
    mixed = lax.psum(partial, "seq")
    middle = stream + rms_scale(mixed, gain_second)
    feed_input = rms_scale(middle, gain_third).astype(jnp.bfloat16)
    block_rows = lax.all_gather(feed_input, "req", axis=0, tiled=True)
    gate_part = jnp.dot(block_rows, gate_weight, preferred_element_type=jnp.float32)
    up_part = jnp.dot(block_rows, up_weight, preferred_element_type=jnp.float32)
    hidden = (jax.nn.gelu(gate_part, approximate=True) * up_part).astype(jnp.bfloat16)
    summed = jnp.dot(hidden, down_weight, preferred_element_type=jnp.float32)
    summed = lax.psum_scatter(summed, "req", scatter_dimension=0, tiled=True)
    summed = lax.psum(summed, "seq")
    results = (middle + rms_scale(summed, gain_fourth)).astype(jnp.bfloat16)
    return results.reshape(STEPS, row_count, width)


MESH = pl.DeviceIdType.MESH
SEQ = 8
REQ = 4
OWNERS = 6
TILE = 8
MIX_CHUNKS = 4
SUM_CHUNKS = 7


def kernel(
    x_ref, cos_ref, sin_ref, owner_ref, g1_ref, g2_ref, g3_ref, g4_ref,
    pw_hbm, ck_hbm, cv_hbm, ow_hbm, gw_hbm, uw_hbm, dw_hbm,
    out_ref,
    pw, ck, cv, ow, gw, uw, dw,
    xs_ref, res_ref, gbuf, bsend, brecv, bzsend, bzrecv, tot_ref, tsend, trecv, csend, crecv, mid_ref, feed, lhs_ref, hid_ref,
    part_ref, e1send, e1recv, e2send, e2recv, e3send, e3recv,
    load_sem, a_send, a_recv, a_fwd, b_send, b_recv, bz_send, bz_recv, t_send, t_recv, c_send, c_recv,
    d_send, d_recv, d_fwd, d2_send, d2_recv, e1_ssem, e1_rsem, e2_ssem, e2_rsem, e3_ssem, e3_rsem,
    f_send, f_recv, f_fwd,
):
    me = lax.axis_index("seq")
    row = lax.axis_index("req")
    width = x_ref.shape[2]
    rows = OWNERS * TILE
    ff = gw.shape[0]
    slots, steps = x_ref.shape[:2]
    across = me + 1 - 2 * lax.rem(me, 2)
    other_core = row + 1 - 2 * lax.rem(row, 2)
    other_y = lax.rem(row + 2, REQ)
    is_owner = (me >= 1) & (me <= OWNERS)
    mine = jnp.minimum(jnp.maximum(me - 1, 0), OWNERS - 1)

    loads = [
        pltpu.make_async_copy(src, dst, load_sem.at[n])
        for n, (src, dst) in enumerate(
            [(pw_hbm.at[:, pl.ds(0, 2 * HD)], pw.at[0]), (ck_hbm, ck), (cv_hbm, cv), (ow_hbm, ow),
             (gw_hbm, gw), (uw_hbm, uw)]
        )
    ]
    loads.append(pltpu.make_async_copy(dw_hbm, dw.at[pl.ds(0, ff)], load_sem.at[6]))
    loads.append(
        pltpu.make_async_copy(pw_hbm.at[:, pl.ds(2 * HD, 2 * HD)], pw.at[1], load_sem.at[7])
    )
    loads[0].start()
    loads[7].start()

    barrier = pltpu.get_barrier_semaphore()
    for d in range(1, SEQ):
        pl.semaphore_signal(
            barrier, inc=1, device_id={"seq": lax.rem(me + d, SEQ)}, device_id_type=MESH
        )
    pl.semaphore_signal(barrier, inc=1, device_id={"req": other_core}, device_id_type=MESH)
    pl.semaphore_signal(barrier, inc=1, device_id={"req": other_y}, device_id_type=MESH)

    def remote(src, dst, send, recv, target):
        return pltpu.make_async_remote_copy(
            src_ref=src, dst_ref=dst, send_sem=send, recv_sem=recv,
            device_id=target, device_id_type=MESH,
        )

    def rms(values, gain):
        mean_square = jnp.mean(values * values, axis=-1, keepdims=True)
        return values * lax.rsqrt(mean_square + epsilon) * gain[None, :]

    for n in range(slots):
        xs_ref[n * steps : (n + 1) * steps, :] = x_ref[n].astype(jnp.float32)
    normed = rms(xs_ref[...], g1_ref[...]).astype(jnp.bfloat16)
    cosine, sine = cos_ref[...], sin_ref[...]
    half = HD // 2
    dw[ff:, :] = jnp.zeros((dw.shape[0] - ff, width), dw.dtype)
    hid_ref[...] = jnp.zeros_like(hid_ref)

    def a_copy(part, k):
        target = lax.rem(me + 2 * k, SEQ) if k else across
        return remote(
            gbuf.at[me, part], gbuf.at[me, part], a_send.at[part, k], a_recv.at[me, part],
            {"seq": target},
        )

    def a_forward(part, k):
        source = lax.rem(me + 2 * k, SEQ)
        return remote(
            gbuf.at[source, part], gbuf.at[source, part], a_fwd.at[part, k - 1],
            a_recv.at[source, part], {"seq": across},
        )

    def a_arrived(source, part):
        remote(
            gbuf.at[source, part], gbuf.at[source, part], a_fwd.at[0, 0],
            a_recv.at[source, part], {"seq": across},
        ).wait_recv()

    for part in range(2):
        loads[7 if part else 0].wait()
        if part:
            for n in range(1, 7):
                loads[n].start()
        projected = jnp.dot(normed, pw[part], preferred_element_type=jnp.float32)
        projected = projected.astype(jnp.bfloat16).astype(jnp.float32)
        for h in range(2):
            a = projected[:, h * HD : h * HD + half]
            b = projected[:, h * HD + half : (h + 1) * HD]
            gbuf[me, part, :, h * HD : h * HD + half] = (a * cosine - b * sine).astype(
                jnp.bfloat16
            )
            gbuf[me, part, :, h * HD + half : (h + 1) * HD] = (b * cosine + a * sine).astype(
                jnp.bfloat16
            )
        if part == 0:
            pl.semaphore_wait(barrier, SEQ + 1)
        for k in (2, 3, 1, 0):
            a_copy(part, k).start()
    for part in range(2):
        for k in range(1, 4):
            a_arrived(lax.rem(me + 2 * k, SEQ), part)
            a_forward(part, k).start()

    loads[1].wait()
    loads[2].wait()
    tokens = ck.shape[0]

    def pair_row(shape, axis):
        index = lax.broadcasted_iota(jnp.int32, shape, axis)
        return jnp.where(index >= rows, index - rows, index)

    owned = owner_ref[...] == pair_row((2 * rows, tokens), 0) // steps
    query_row = pair_row((2 * rows, rows), 0)
    fresh_row = lax.broadcasted_iota(jnp.int32, (2 * rows, rows), 1)
    fresh_allowed = (query_row // steps == fresh_row // steps) & (fresh_row <= query_row)
    lanes = lax.broadcasted_iota(jnp.int32, (2 * rows, 128), 1)
    totals = jnp.zeros((2 * rows, 128), jnp.float32)

    def attend(queries, keys, values, allowed):
        scores = lax.dot_general(
            queries, keys, (((1,), (1,)), ((), ())), preferred_element_type=jnp.float32
        )
        weights = jnp.where(allowed, capped_weight(scores), 0.0)
        outputs = jnp.dot(
            weights.astype(jnp.bfloat16), values, preferred_element_type=jnp.float32
        )
        return jnp.sum(weights, axis=-1, keepdims=True), outputs

    def b_copy(k):
        return remote(bsend.at[k], brecv.at[k], b_send.at[k], b_recv.at[k], {"seq": across})

    def bz_copy(k):
        return remote(
            bzsend.at[k - 1], bzrecv.at[k - 1], bz_send.at[k - 1], bz_recv.at[k - 1],
            {"seq": lax.rem(me + 2 * k, SEQ)},
        )

    def t_copy(j):
        return remote(
            tsend, trecv.at[j - 1], t_send.at[j - 1], t_recv.at[j - 1],
            {"seq": lax.rem(me + j, SEQ)},
        )

    for side, k in [(across, 2), (across, 3), (across, 1), (across, 0),
                    (me, 2), (me, 3), (me, 1), (me, 0)]:
        e = lax.rem(side + 2 * k, SEQ)
        block = e // 2
        part = lax.rem(e, 2)

        @pl.when(lax.rem(block, 2) != lax.rem(me, 2))
        def _():
            a_arrived(block, part)

        queries = jnp.concatenate([gbuf[block, part, :, :HD], gbuf[block, part, :, HD:]], axis=0)
        head = pl.ds(pl.multiple_of(e * HD, HD), HD)
        total, outputs = attend(queries, ck[:, head], cv[:, head], owned)
        if side is across:
            bsend[k] = outputs.astype(jnp.bfloat16)
            b_copy(k).start()
        elif k:
            b_copy(k).wait_recv()
            bzsend[k - 1] = (outputs + brecv[k].astype(jnp.float32)).astype(jnp.bfloat16)
            bz_copy(k).start()
        else:
            for n in range(SEQ // 2, SEQ):
                @pl.when(n % 2 != lax.rem(me, 2))
                def _():
                    a_arrived(n, 0)
                    a_arrived(n, 1)

            home, lane = lax.rem(e // 2, 2), pl.ds(pl.multiple_of(lax.rem(e, 2) * HD, HD), HD)
            fresh_total, fresh_outputs = attend(
                queries, gbuf[4 + e // 4, home, :, lane], gbuf[6 + e // 4, home, :, lane],
                fresh_allowed,
            )
            total = total + fresh_total
            outputs = outputs + fresh_outputs
        totals = totals + jnp.where(lanes == e, total, 0.0)
    tot_ref[2 * rows :, :] = jnp.zeros((128 - 2 * rows, 128), jnp.float32)
    tot_ref[: 2 * rows, :] = totals
    tsend[...] = tot_ref[...].T[:KVH]
    for j in range(1, SEQ):
        t_copy(j).start()
    everyone = tsend[...]
    b_copy(0).wait_recv()
    outputs = outputs + brecv[0].astype(jnp.float32)
    for k in range(1, 4):
        bz_copy(k).wait_recv()
        outputs = outputs + bzrecv[k - 1].astype(jnp.float32)
    for j in range(1, SEQ):
        t_copy(j).wait_recv()
        everyone = everyone + trecv[j - 1]
    tot_ref[...] = jnp.zeros((128, 128), jnp.float32)
    tot_ref[:KVH, :] = everyone
    spread = tot_ref[...].T
    column = jnp.sum(jnp.where(lanes == me, spread[: 2 * rows], 0.0), axis=-1, keepdims=True)
    attended = outputs / column
    attended = jnp.concatenate([attended[:rows], attended[rows:]], axis=1).astype(jnp.bfloat16)

    loads[3].wait()
    mix = width // MIX_CHUNKS

    def c_send_to(c, d):
        target = lax.rem(me + d, SEQ)
        owner = jnp.minimum(jnp.maximum(target - 1, 0), OWNERS - 1)
        copy = remote(
            csend.at[c, owner], crecv.at[c, d - 1], c_send.at[c, d - 1], c_recv.at[c, d - 1],
            {"seq": target},
        )
        return (target >= 1) & (target <= OWNERS), copy

    for c in range(MIX_CHUNKS):
        part = jnp.dot(
            attended, ow[:, c * mix : (c + 1) * mix], preferred_element_type=jnp.float32
        )
        csend[c] = part.reshape(OWNERS, TILE, mix).astype(jnp.bfloat16)
        for d in range(1, SEQ):
            pred, copy = c_send_to(c, d)
            pl.when(pred)(copy.start)

    def d_copy(k):
        target = lax.rem(me + 2 * k, SEQ) if k else across
        return remote(
            feed.at[0, mine], feed.at[0, mine], d_send.at[k], d_recv.at[mine], {"seq": target}
        )

    def owner_of(seq):
        valid = (seq >= 1) & (seq <= OWNERS)
        return valid, jnp.minimum(jnp.maximum(seq - 1, 0), OWNERS - 1)

    def d_forward(k):
        valid, o = owner_of(lax.rem(me + 2 * k, SEQ))
        return valid, o, remote(
            feed.at[0, o], feed.at[0, o], d_fwd.at[k - 1], d_recv.at[o], {"seq": across}
        )

    @pl.when(is_owner)
    def _():
        pieces = []
        for c in range(MIX_CHUNKS):
            piece = csend[c, mine].astype(jnp.float32)
            for d in range(1, SEQ):
                c_send_to(c, d)[1].wait_recv()
                piece = piece + crecv[c, d - 1].astype(jnp.float32)
            pieces.append(piece)
        mixed = jnp.concatenate(pieces, axis=1)
        middle = xs_ref[pl.ds(pl.multiple_of(mine * TILE, TILE), TILE), :] + rms(mixed, g2_ref[...])
        mid_ref[...] = middle
        feed[0, mine] = rms(middle, g3_ref[...]).astype(jnp.bfloat16)
        for k in (2, 3, 1, 0):
            d_copy(k).start()

    def to_y(o):
        return remote(
            feed.at[0, o], feed.at[2, o], d2_send.at[0, o], d2_recv.at[0, o], {"req": other_y}
        )

    def to_core(o):
        return remote(
            feed.at[0, o], feed.at[1, o], d2_send.at[1, o], d2_recv.at[1, o], {"req": other_core}
        )

    def to_corner(o):
        return remote(
            feed.at[2, o], feed.at[3, o], d2_send.at[2, o], d2_recv.at[2, o], {"req": other_core}
        )

    def fill(q):
        lhs_ref[q * rows : (q + 1) * rows, :] = (
            feed[q].astype(jnp.float32).reshape(rows, width).astype(jnp.bfloat16)
        )

    def feed_half(n):
        block = lhs_ref[n * 2 * rows : (n + 1) * 2 * rows, :]
        nt = (((1,), (1,)), ((), ()))
        gate_part = lax.dot_general(block, gw[...], nt, preferred_element_type=jnp.float32)
        up_part = lax.dot_general(block, uw[...], nt, preferred_element_type=jnp.float32)
        hidden = (jax.nn.gelu(gate_part, approximate=True) * up_part).astype(jnp.bfloat16)
        hid_ref[n * 2 * rows : (n + 1) * 2 * rows, :ff] = hidden

    @pl.when(is_owner)
    def _():
        to_y(mine).start()
        to_core(mine).start()

    for k in range(1, 4):
        valid, o, copy = d_forward(k)

        @pl.when(valid)
        def _():
            copy.wait_recv()
            copy.start()
            to_y(o).start()
            to_core(o).start()

    for k in range(4):
        valid, o = owner_of(lax.rem(across + 2 * k, SEQ))

        @pl.when(valid)
        def _():
            remote(
                feed.at[0, o], feed.at[0, o], d_fwd.at[0], d_recv.at[o], {"seq": across}
            ).wait_recv()
            to_y(o).start()
            to_core(o).start()

    fill(0)
    for o in range(OWNERS):
        to_core(o).wait_recv()
    fill(1)
    loads[4].wait()
    loads[5].wait()
    feed_half(0)
    for o in range(OWNERS):
        to_y(o).wait_recv()
        to_corner(o).start()
    fill(2)
    for o in range(OWNERS):
        to_corner(o).wait_recv()
    fill(3)
    feed_half(1)
    loads[6].wait()
    piece_width = width // SUM_CHUNKS

    def e1_copy(c):
        return remote(
            e1send.at[c], e1recv.at[c], e1_ssem.at[c], e1_rsem.at[c], {"req": other_core}
        )

    def e2_copy(c):
        return remote(e2send.at[c], e2recv.at[c], e2_ssem.at[c], e2_rsem.at[c], {"req": other_y})

    def e3_copy(c, d):
        target = lax.rem(me + d, SEQ)
        owner = jnp.minimum(jnp.maximum(target - 1, 0), OWNERS - 1)
        copy = remote(
            e3send.at[c, owner], e3recv.at[c, d - 1], e3_ssem.at[c, d - 1], e3_rsem.at[c, d - 1],
            {"seq": target},
        )
        return (target >= 1) & (target <= OWNERS), copy

    for c in range(SUM_CHUNKS):
        part = jnp.dot(
            hid_ref[...],
            dw[:, c * piece_width : (c + 1) * piece_width],
            preferred_element_type=jnp.float32,
        )
        e1send[c, :rows] = part[rows : 2 * rows].astype(jnp.bfloat16)
        e1send[c, rows:] = part[3 * rows :].astype(jnp.bfloat16)
        part_ref[c, :rows] = part[:rows]
        part_ref[c, rows:] = part[2 * rows : 3 * rows]
        e1_copy(c).start()
    for c in range(SUM_CHUNKS):
        e1_copy(c).wait_recv()
        e2send[c] = (part_ref[c, rows:] + e1recv[c, rows:].astype(jnp.float32)).astype(
            jnp.bfloat16
        )
        e2_copy(c).start()
    for c in range(SUM_CHUNKS):
        e2_copy(c).wait_recv()
        kept = part_ref[c, :rows] + e1recv[c, :rows].astype(jnp.float32)
        kept = kept + e2recv[c].astype(jnp.float32)
        e3send[c] = kept.reshape(OWNERS, TILE, piece_width).astype(jnp.bfloat16)
        for d in range(1, SEQ):
            pred, copy = e3_copy(c, d)
            pl.when(pred)(copy.start)

    def f_copy(k):
        target = lax.rem(me + 2 * k, SEQ) if k else across
        return remote(
            res_ref.at[mine], res_ref.at[mine], f_send.at[k], f_recv.at[mine], {"seq": target}
        )

    def f_forward(k):
        valid, o = owner_of(lax.rem(me + 2 * k, SEQ))
        return valid, remote(
            res_ref.at[o], res_ref.at[o], f_fwd.at[k - 1], f_recv.at[o], {"seq": across}
        )

    @pl.when(is_owner)
    def _():
        pieces = []
        for c in range(SUM_CHUNKS):
            piece = e3send[c, mine].astype(jnp.float32)
            for d in range(1, SEQ):
                e3_copy(c, d)[1].wait_recv()
                piece = piece + e3recv[c, d - 1].astype(jnp.float32)
            pieces.append(piece)
        summed = jnp.concatenate(pieces, axis=1)
        res_ref[mine] = (mid_ref[...] + rms(summed, g4_ref[...])).astype(jnp.bfloat16)
        for k in (2, 3, 1, 0):
            f_copy(k).start()

    for k in range(1, 4):
        valid, copy = f_forward(k)

        @pl.when(valid)
        def _():
            copy.wait_recv()
            copy.start()

    for k in range(4):
        valid, o = owner_of(lax.rem(across + 2 * k, SEQ))

        @pl.when(valid)
        def _():
            remote(
                res_ref.at[o], res_ref.at[o], f_fwd.at[0], f_recv.at[o], {"seq": across}
            ).wait_recv()

    finished = res_ref[...].astype(jnp.float32).reshape(rows, width)
    for n in range(slots):
        out_ref[n] = finished[n * steps : (n + 1) * steps].astype(jnp.bfloat16)

    for d in range(1, SEQ):
        t_copy(d).wait_send()
        for c in range(MIX_CHUNKS):
            pred, copy = c_send_to(c, d)
            pl.when(pred)(copy.wait_send)
        for c in range(SUM_CHUNKS):
            pred, copy = e3_copy(c, d)
            pl.when(pred)(copy.wait_send)
    for k in range(4):
        b_copy(k).wait_send()
    for k in range(1, 4):
        bz_copy(k).wait_send()
    for part in range(2):
        for k in range(4):
            a_copy(part, k).wait_send()
        for k in range(1, 4):
            a_forward(part, k).wait_send()
    for k in range(1, 4):
        valid, _o, copy = d_forward(k)
        pl.when(valid)(copy.wait_send)
        valid, copy = f_forward(k)
        pl.when(valid)(copy.wait_send)
    for o in range(OWNERS):
        to_y(o).wait_send()
        to_core(o).wait_send()
        to_corner(o).wait_send()
    for c in range(SUM_CHUNKS):
        e1_copy(c).wait_send()
        e2_copy(c).wait_send()

    @pl.when(is_owner)
    def _():
        for k in range(4):
            d_copy(k).wait_send()
            f_copy(k).wait_send()


def fused_body(
    embedded,
    cache_keys,
    cache_values,
    token_owner,
    dealing,
    lengths,
    project_weight,
    output_weight,
    gate_weight,
    up_weight,
    down_weight,
    gain_first,
    gain_second,
    gain_third,
    gain_fourth,
):
    row_count = embedded.shape[1]
    rows = STEPS * row_count
    width = embedded.shape[2]
    tokens = cache_keys.shape[1]
    kvw = cache_keys.shape[2]
    columns = project_weight.shape[1]
    depth = output_weight.shape[0]
    ff = gate_weight.shape[1]
    ff_pad = -(-ff // 128) * 128
    mix = width // MIX_CHUNKS
    piece = width // SUM_CHUNKS
    group_index = lax.axis_index("req")
    seq_index = lax.axis_index("seq")
    slot_requests = lax.dynamic_slice_in_dim(dealing, group_index * row_count, row_count)
    matches = slot_requests[:, None] == jnp.arange(dealing.shape[0], dtype=jnp.int32)[None, :]
    base_positions = jnp.sum(jnp.where(matches, lengths[None, :], 0), axis=1)
    positions = base_positions[:, None] + jnp.arange(STEPS, dtype=jnp.int32)[None, :]
    positions = positions.reshape(rows).astype(jnp.float32)
    freq_index = jnp.arange(HD // 2, dtype=jnp.float32)
    inverse = jnp.exp(freq_index * (-2.0 * math.log(10000.0) / HD))
    angles = positions[:, None] * inverse[None, :]
    scale = jnp.where(seq_index < SEQ // 2, HD ** (-0.5), 1.0)
    turned = seq_index < 3 * SEQ // 4
    cosine = jnp.where(turned, jnp.cos(angles) * scale, 1.0)
    sine = jnp.where(turned, jnp.sin(angles) * scale, 0.0)
    bf16, f32 = jnp.bfloat16, jnp.float32
    dma = pltpu.SemaphoreType.DMA
    vmem = pl.BlockSpec(memory_space=pltpu.VMEM)
    hbm = pl.BlockSpec(memory_space=pl.ANY)
    out = pl.pallas_call(
        kernel,
        out_shape=jax.ShapeDtypeStruct((row_count, STEPS, width), bf16),
        in_specs=[vmem] * 8 + [hbm] * 7,
        out_specs=vmem,
        scratch_shapes=[
            pltpu.VMEM((2, width, columns // 2), bf16),
            pltpu.VMEM((tokens, kvw), bf16),
            pltpu.VMEM((tokens, kvw), bf16),
            pltpu.VMEM((depth, width), bf16),
            pltpu.VMEM((ff, width), bf16),
            pltpu.VMEM((ff, width), bf16),
            pltpu.VMEM((ff_pad, width), bf16),
            pltpu.VMEM((rows, width), f32),
            pltpu.VMEM((OWNERS, TILE, width), bf16),
            pltpu.VMEM((SEQ, 2, rows, columns // 2), bf16),
            pltpu.VMEM((4, 2 * rows, HD), bf16),
            pltpu.VMEM((4, 2 * rows, HD), bf16),
            pltpu.VMEM((3, 2 * rows, HD), bf16),
            pltpu.VMEM((3, 2 * rows, HD), bf16),
            pltpu.VMEM((128, 128), f32),
            pltpu.VMEM((KVH, 128), f32),
            pltpu.VMEM((SEQ - 1, KVH, 128), f32),
            pltpu.VMEM((MIX_CHUNKS, OWNERS, TILE, mix), bf16),
            pltpu.VMEM((MIX_CHUNKS, SEQ - 1, TILE, mix), bf16),
            pltpu.VMEM((TILE, width), f32),
            pltpu.VMEM((REQ, OWNERS, TILE, width), bf16),
            pltpu.VMEM((REQ * rows, width), bf16),
            pltpu.VMEM((REQ * rows, ff_pad), bf16),
            pltpu.VMEM((SUM_CHUNKS, 2 * rows, piece), f32),
            pltpu.VMEM((SUM_CHUNKS, 2 * rows, piece), bf16),
            pltpu.VMEM((SUM_CHUNKS, 2 * rows, piece), bf16),
            pltpu.VMEM((SUM_CHUNKS, rows, piece), bf16),
            pltpu.VMEM((SUM_CHUNKS, rows, piece), bf16),
            pltpu.VMEM((SUM_CHUNKS, OWNERS, TILE, piece), bf16),
            pltpu.VMEM((SUM_CHUNKS, SEQ - 1, TILE, piece), bf16),
            dma((8,)),
            dma((2, 4)),
            dma((SEQ, 2)),
            dma((2, 3)),
            dma((4,)),
            dma((4,)),
            dma((3,)),
            dma((3,)),
            dma((SEQ - 1,)),
            dma((SEQ - 1,)),
            dma((MIX_CHUNKS, SEQ - 1)),
            dma((MIX_CHUNKS, SEQ - 1)),
            dma((4,)),
            dma((OWNERS,)),
            dma((3,)),
            dma((3, OWNERS)),
            dma((3, OWNERS)),
            dma((SUM_CHUNKS,)),
            dma((SUM_CHUNKS,)),
            dma((SUM_CHUNKS,)),
            dma((SUM_CHUNKS,)),
            dma((SUM_CHUNKS, SEQ - 1)),
            dma((SUM_CHUNKS, SEQ - 1)),
            dma((4,)),
            dma((OWNERS,)),
            dma((3,)),
        ],
        compiler_params=pltpu.CompilerParams(
            collective_id=0, has_side_effects=True, vmem_limit_bytes=58 << 20
        ),
    )(
        embedded.transpose(1, 0, 2),
        cosine,
        sine,
        token_owner,
        gain_first,
        gain_second,
        gain_third,
        gain_fourth,
        project_weight,
        cache_keys[0],
        cache_values[0],
        output_weight,
        gate_weight.T,
        up_weight.T,
        down_weight,
    )
    return out.transpose(1, 0, 2)


def body(*args):
    embedded, cache_keys = args[0], args[1]
    rows = STEPS * embedded.shape[1]
    fits = (
        lax.axis_size("seq") == SEQ
        and lax.axis_size("req") == REQ
        and rows == OWNERS * TILE
        and KVH == SEQ
        and cache_keys.shape[2] == KVH * HD
    )
    return fused_body(*args) if fits else plain_body(*args)


def solution(mesh):
    return jax.shard_map(
        body,
        mesh=mesh,
        in_specs=(
            P(None, "req", None),
            P("req", "seq", None),
            P("req", "seq", None),
            P("req", "seq"),
            P(),
            P(),
            P(None, "seq"),
            P("seq", None),
            P(None, ("req", "seq")),
            P(None, ("req", "seq")),
            P(("req", "seq"), None),
            P(),
            P(),
            P(),
            P(),
        ),
        out_specs=P(None, "req", None),
        check_vma=False,
    )
```
